256 devices in a mesh: dp: 2 (over x_hi), lat: 16 (over x_lo, z), lon: 8 (over y, core).
Axes of the slice: x: 4 (x_hi: 2, x_lo: 2; x = x_hi * 2 + x_lo), y: 4, z: 8, core: 2. Of those that a mesh axis runs over, the one named last changes fastest.
Arguments:
- hidden_in: bfloat16 [2, 480, 480, 384], P('dp', 'lat', 'lon'), may hold values from -6 to 6
- grad_out: bfloat16 [2, 480, 480, 384], P('dp', 'lat', 'lon'), may hold values from -6 to 6
- norm_gain: float32 [384], replicated, may hold values from 0.5 to 1.5
- w_qkv: bfloat16 [384, 1152], replicated, may hold values from -0.3125 to 0.3125
- w_proj: bfloat16 [384, 384], replicated, may hold values from -0.3125 to 0.3125
Outputs:
- grad_in: bfloat16 [2, 480, 480, 384], P('dp', 'lat', 'lon')
- grad_qkv: float32 [384, 1152], P('dp', ('lat', 'lon'))
- grad_proj: float32 [384, 384], P('dp', ('lat', 'lon'))
The draws below stay inside these ranges and needn't reach their ends.
All inputs are finite; a program needn't handle non-finite values.
Results may differ from the reference program's by a relative error of at most 0.0083.
Values may be sent and summed in bfloat16 or wider, within the bound.
A program may use at most 64 MiB of HBM per device.

```python
import jax
import jax.numpy as jnp
from jax import lax

D = 384
HEADS = 6
WIN = 30
SHIFT = 15
BATCH = 2
NLAT = 480
NLON = 480
CELLS = 460800


def steps_of(key, shape, cuts, low, top_value):
    loudness = 1.0
    for axis_at, shards_of in cuts:
        heights = jax.random.uniform(jax.random.fold_in(jax.random.fold_in(key, 6), axis_at), (shards_of,), jnp.float32, low / len(cuts), top_value / len(cuts))
        loudness = loudness * jnp.repeat(jnp.exp(heights), shape[axis_at] // shards_of).reshape((-1,) + (1,) * (len(shape) - 1 - axis_at))
    return loudness


def noise(own_key, shape, spread, most, shards=(), kind=jnp.bfloat16):
    array = jax.random.normal(own_key, shape, jnp.float32) * spread
    if len(shards) > 0:
        array = steps_of(own_key, shape, shards, -0.22, 0.18) * array
    return jnp.clip(array, min=-most, max=most).astype(kind)


def setup_inputs(seed: int = 0) -> dict:
    splits = jax.random.split(jax.random.key(seed), 6)
    hidden_in = noise(splits[0], (BATCH, NLAT, NLON, D), 1.0, 6.0, ((0, 2), (1, 16), (2, 8)))
    grad_out = noise(splits[1], (BATCH, NLAT, NLON, D), 1.0, 6.0, ((0, 2), (1, 16), (2, 8)))
    norm_gain = jnp.clip(1.0 + 0.1 * jax.random.normal(splits[2], (D,), jnp.float32), 0.5, 1.5)
    w_qkv = noise(splits[3], (D, 3 * D), D ** -0.5, 0.3125)
    w_proj = noise(splits[4], (D, D), D ** -0.5, 0.3125)
    return {"hidden_in": hidden_in, "grad_out": grad_out, "norm_gain": norm_gain, "w_qkv": w_qkv, "w_proj": w_proj}


EPSILON = 1e-05

def attend_head(query_rows, key_rows, value_rows, grad_rows, key_valid, scaling):
    scores = jnp.dot(query_rows, key_rows.T, preferred_element_type=jnp.float32) * scaling
    weights_raw = jnp.exp(scores) * key_valid[None, :]
    attention = weights_raw / lax.optimization_barrier(jnp.sum(weights_raw, axis=-1, keepdims=True))
    attention_low = attention.astype(jnp.bfloat16)
    outputs = jnp.dot(attention_low, value_rows, preferred_element_type=jnp.float32).astype(jnp.bfloat16)
    dprobs = jnp.dot(grad_rows, value_rows.T, preferred_element_type=jnp.float32)
    row_total = lax.optimization_barrier(jnp.sum(attention * dprobs, axis=-1, keepdims=True))
    dscores = (attention * (dprobs - row_total) * scaling).astype(jnp.bfloat16)
    dquery = jnp.dot(dscores, key_rows, preferred_element_type=jnp.float32).astype(jnp.bfloat16)
    dkey_rows = jnp.dot(dscores.T, query_rows, preferred_element_type=jnp.float32).astype(jnp.bfloat16)
    dvalue = jnp.dot(attention_low.T, grad_rows, preferred_element_type=jnp.float32).astype(jnp.bfloat16)
    return (outputs, dquery, dkey_rows, dvalue)

def window_grads(window_cells, cotangent, key_valid, norm_gain, w_qkv, w_proj):
    model_width = window_cells.shape[1]
    head_size = model_width // HEADS
    scaling = head_size ** (-0.5)
    values_f = window_cells.astype(jnp.float32)
    average = lax.optimization_barrier(jnp.mean(values_f, axis=1, keepdims=True))
    centred = values_f - average
    inverse_std = lax.rsqrt(lax.optimization_barrier(jnp.mean(centred * centred, axis=1, keepdims=True)) + EPSILON)
    normed = centred * inverse_std
    normal_low = (normed * norm_gain).astype(jnp.bfloat16)
    qkv = jnp.dot(normal_low, w_qkv, preferred_element_type=jnp.float32).astype(jnp.bfloat16)
    back_rows = jnp.dot(cotangent, w_proj.T, preferred_element_type=jnp.float32).astype(jnp.bfloat16)

    def split_heads(matrix):
        return matrix.reshape(matrix.shape[0], HEADS, head_size).transpose(1, 0, 2)

    def merge_heads(stacked):
        return stacked.transpose(1, 0, 2).reshape(stacked.shape[1], model_width)

    def one_head(inputs):
        return attend_head(inputs[0], inputs[1], inputs[2], inputs[3], key_valid, scaling)
    heads_in = (split_heads(qkv[:, :model_width]), split_heads(qkv[:, model_width:2 * model_width]), split_heads(qkv[:, 2 * model_width:]), split_heads(back_rows))
    outputs, dquery, dkey_rows, dvalue = lax.map(one_head, heads_in)
    attended = merge_heads(outputs)
    dqkv = jnp.concatenate([merge_heads(dquery), merge_heads(dkey_rows), merge_heads(dvalue)], axis=1)
    proj_part = jnp.dot(attended.T, cotangent, preferred_element_type=jnp.float32)
    qkv_part = jnp.dot(normal_low.T, dqkv, preferred_element_type=jnp.float32)
    dnormed = jnp.dot(dqkv, w_qkv.T, preferred_element_type=jnp.float32) * norm_gain
    dcells = inverse_std * (dnormed - lax.optimization_barrier(jnp.mean(dnormed, axis=1, keepdims=True)) - normed * lax.optimization_barrier(jnp.mean(dnormed * normed, axis=1, keepdims=True)))
    return (dcells.astype(jnp.bfloat16), qkv_part, proj_part)

def to_windows(grid_field):
    shape = grid_field.shape
    split = grid_field.reshape(shape[0], shape[1] // WIN, WIN, shape[2] // WIN, WIN, shape[3])
    return split.transpose(0, 1, 3, 2, 4, 5).reshape(-1, WIN * WIN, shape[3])

def from_windows(windows, samples, lat_rows, lon_cols):
    split = windows.reshape(samples, lat_rows // WIN, lon_cols // WIN, WIN, WIN, windows.shape[-1])
    return split.transpose(0, 1, 3, 2, 4, 5).reshape(samples, lat_rows, lon_cols, windows.shape[-1])

def shift_ahead(grid_field):
    rolled = jnp.roll(grid_field, -SHIFT, axis=2)
    padding = jnp.zeros_like(rolled[:, :SHIFT])
    return jnp.concatenate([rolled[:, SHIFT:], padding], axis=1)

def shift_behind(grid_field):
    rolled = jnp.roll(grid_field, SHIFT, axis=2)
    padding = jnp.zeros_like(rolled[:, :SHIFT])
    return jnp.concatenate([padding, rolled[:, :-SHIFT]], axis=1)

def reference(hidden_in, grad_out, norm_gain, w_qkv, w_proj):
    shifted = shift_ahead(hidden_in)
    cotangent = shift_ahead(grad_out)
    row_index = jnp.arange(NLAT, dtype=jnp.int32)
    valid_rows = (row_index < NLAT - SHIFT).astype(jnp.float32)
    valid_field = jnp.broadcast_to(valid_rows[None, :, None, None], (BATCH, NLAT, NLON, 1))
    valid_windows = to_windows(valid_field)[..., 0]

    def step_window(totals, inputs):
        dcells, qkv_part, proj_part = window_grads(inputs[0], inputs[1], inputs[2], norm_gain, w_qkv, w_proj)
        return ((totals[0] + qkv_part, totals[1] + proj_part), dcells)
    starting = (jnp.zeros((D, 3 * D), jnp.float32), jnp.zeros((D, D), jnp.float32))
    sums, dwindows = lax.scan(step_window, starting, (to_windows(shifted), to_windows(cotangent), valid_windows))
    dshift = from_windows(dwindows, BATCH, NLAT, NLON)
    returned = shift_behind(dshift)
    grad_in = (grad_out.astype(jnp.float32) + returned.astype(jnp.float32)).astype(jnp.bfloat16)
    factor = float(CELLS) ** (-0.5)
    return (grad_in, sums[0] * factor, sums[1] * factor)
```

```python
import functools
import jax, jax.numpy as jnp
from jax import lax
from jax.experimental import pallas as pl
from jax.experimental.pallas import tpu as pltpu
from jax.sharding import Mesh
from jax.sharding import PartitionSpec as P
HEADS=6; D=384; HD=64; EPS=1e-5
KC=960; QC=1024; QT=256
BF=bf=jnp.bfloat16
F32=f32=jnp.float32
MESH=pl.DeviceIdType.MESH
NN=(((1,),(0,)),((),())); NT=(((1,),(1,)),((),()))
def dot(a,b,dims=NN): return lax.dot_general(a,b,dims,preferred_element_type=f32)

def window_kernel(group, flag_ref, x_ref, g_ref, gain_ref, wqkv_ref, wqkvT_ref, wp_ref,
                  d_ref, gq_ref, gp_ref,
                  normed, rstd_s, nl, gs, qTa, bTa, kaug, vaug, qkvT, P32, PT, DST, dqkvT, attT):
    gain=gain_ref[...]
    CH=128
    def ln(i,c):
        rows=pl.ds(pl.multiple_of(i*CH,CH),CH)
        x=x_ref[rows,:].astype(f32)
        mu=jnp.sum(x,axis=1,keepdims=True)*(1/D)
        xc=x-mu
        var=jnp.sum(xc*xc,axis=1,keepdims=True)*(1/D)
        rs=lax.rsqrt(var+EPS)
        n=xc*rs
        normed[rows,:]=n
        rstd_s[rows,:]=jnp.broadcast_to(rs,(CH,128))
        nl[rows,:]=(n*gain).astype(bf)
        return c
    lax.fori_loop(0,QC//CH,ln,0)
    zero=jnp.zeros((64,QC),bf)
    for h in range(HEADS):
        o=(h%2)*64
        qh=dot(wqkvT_ref[h*64:(h+1)*64,:],nl[...],NT).astype(bf)
        qkvT[h]=qh
        qTa[h,o:o+64,:]=qh
        qTa[h,64-o:128-o,:]=zero
        bh=dot(wp_ref[h*64:(h+1)*64,:],g_ref[...],NT).astype(bf)
        bTa[h,o:o+64,:]=bh
        bTa[h,64-o:128-o,:]=zero
        one=(lax.broadcasted_iota(jnp.int32,(128,QC),0)==0).astype(f32).astype(bf)
        qTa[h,128:256,:]=one
        bTa[h,128:256,:]=jnp.zeros((128,QC),bf)
    for h in range(HEADS,3*HEADS):
        qkvT[h]=dot(wqkvT_ref[h*64:(h+1)*64,:],nl[...],NT).astype(bf)
    row=lax.broadcasted_iota(jnp.int32,(KC,128),0)
    lane=lax.broadcasted_iota(jnp.int32,(KC,128),1)
    bad=(lax.rem(row,group)>=group-group//15)|((row>=KC//2)&(flag_ref[0]==0))
    bias=jnp.where((lane==0)&bad,-30000.0,0.0).astype(bf)
    ones=jnp.where(lane<2,1.0,0.0).astype(bf)
    for j in range(3):
        kaug[j,:,0:128]=dot(nl[0:KC,:],wqkv_ref[:,D+j*128:D+(j+1)*128]).astype(bf)
        vaug[j,:,0:128]=dot(nl[0:KC,:],wqkv_ref[:,2*D+j*128:2*D+(j+1)*128]).astype(bf)
        kaug[j,:,128:256]=bias
        vaug[j,:,128:256]=ones
    CK=240
    def head(h,c):
        j=h//2
        o=pl.multiple_of((h%2)*64,64)
        for t in range(QC//QT):
            ts=slice(t*QT,(t+1)*QT)
            acc=jnp.zeros((8,QT),f32)
            for k in range(0,KC,CK):
                e=jnp.exp(dot(kaug[j,k:k+CK,:],qTa[h,:,ts]))
                P32[k:k+CK,ts]=e
                acc=acc+jnp.sum(e.reshape(CK//8,8,QT),axis=0)
            r=1.0/jnp.sum(acc,axis=0,keepdims=True)
            for k in range(0,KC,CK):
                p=P32[k:k+CK,ts]*r
                P32[k:k+CK,ts]=p
                PT[k:k+CK,ts]=p.astype(bf)
            a=dot(qkvT[12+h][:,0:KC],PT[:,ts])
            attT[h,:,ts]=a.astype(bf)
            nd=-jnp.sum(a*bTa[h,pl.ds(o,64),ts].astype(f32),axis=0,keepdims=True)
            hi=nd.astype(bf).astype(f32)
            lo=nd-hi
            r16=lax.broadcasted_iota(jnp.int32,(16,QT),0)
            bTa[h,128:144,ts]=jnp.where(r16==0,hi,jnp.where(r16==1,lo,0.0)).astype(bf)
            for k in range(0,KC,CK):
                dp=dot(vaug[j,k:k+CK,:],bTa[h,:,ts])
                DST[k:k+CK,ts]=(P32[k:k+CK,ts]*dp).astype(bf)
            dqkvT[h,:,ts]=dot(qkvT[6+h][:,0:KC],DST[:,ts]).astype(bf)
        dqkvT[6+h,:,0:KC]=dot(qkvT[h],DST[...],NT).astype(bf)
        dqkvT[12+h,:,0:KC]=dot(bTa[h,pl.ds(o,64),:],PT[...],NT).astype(bf)
        return c
    dqkvT[:,:,KC:]=jnp.zeros((18,64,QC-KC),bf)
    lax.fori_loop(0,HEADS,head,0)
    dall=dqkvT[...].reshape(3*D,QC)
    gq_ref[...]=dot(dall,nl[...])
    gp_ref[...]=dot(attT[...].reshape(D,QC),g_ref[...])
    for t in range(QC//QT):
        rows=slice(t*QT,(t+1)*QT)
        dn=dot(wqkv_ref[...],dqkvT[:,:,rows].reshape(3*D,QT)).T*gain
        n=normed[rows,:]
        m1=jnp.sum(dn,axis=1,keepdims=True)*(1/D)
        m2=jnp.sum(dn*n,axis=1,keepdims=True)*(1/D)
        d_ref[rows,:]=(rstd_s[rows,0:1]*(dn-m1-n*m2)).astype(bf)

def window_call(group, flag, x, g, gain, wqkv, wqkvT, wp):
    V=pl.BlockSpec(memory_space=pltpu.VMEM)
    return pl.pallas_call(
        functools.partial(window_kernel,group),
        out_shape=(jax.ShapeDtypeStruct((QC,D),bf),jax.ShapeDtypeStruct((3*D,D),f32),jax.ShapeDtypeStruct((D,D),f32)),
        in_specs=[pl.BlockSpec(memory_space=pltpu.SMEM)]+[V]*6,
        out_specs=(V,V,V),
        scratch_shapes=[pltpu.VMEM(s,d) for s,d in [((QC,D),f32),((QC,128),f32),((QC,D),bf),((8,128),bf),
            ((6,256,QC),bf),((6,256,QC),bf),((3,KC,256),bf),((3,KC,256),bf),((18,64,QC),bf),
            ((KC,QC),f32),((KC,QC),bf),((KC,QC),bf),((18,64,QC),bf),((6,64,QC),bf)]],
        compiler_params=pltpu.CompilerParams(vmem_limit_bytes=60*1024*1024),
        cost_estimate=pl.CostEstimate(flops=8*10**9,bytes_accessed=10**7,transcendentals=6*10**6),
        name="window_grads",
    )(flag, x, g, gain, wqkv, wqkvT, wp)


def reduce_kernel(gqa, gqb, gpa, gpb, out, total, core_send, core_recv, core_own, y_send, y_recv, y_own,
                  lat_send, lat_recv, dp_send, dp_recv, send_sems, recv_sems):
    xl, z, y, core = (lax.axis_index(n) for n in ("xl", "z", "y", "core"))
    dp = lax.axis_index("dp")
    lat = xl * 8 + z

    def lat_peer(k):
        t = lax.rem(lat + k, 16)
        return t, {"xl": t // 8, "z": lax.rem(t, 8)}

    barrier = pltpu.get_barrier_semaphore()
    peers = [{"core": 1 - core}, {"dp": 1 - dp}]
    peers += [{"y": lax.rem(y + k, 4)} for k in range(1, 4)]
    peers += [lat_peer(k)[1] for k in range(1, 16)]
    for peer in peers:
        pl.semaphore_signal(barrier, inc=1, device_id=peer, device_id_type=MESH)

    for n in range(3):
        total[n, 0:1152, :] = gqa[:, n * 128:(n + 1) * 128] + gqb[:, n * 128:(n + 1) * 128]
        rows = slice(n * 128, (n + 1) * 128)
        total[n, 1152:1536, :] = (gpa[rows, :] + gpb[rows, :]).T

    def gather(lon, j):
        first, step = (9 * lon + j, 72) if j < 9 else (1152 + 3 * lon + j - 9, 24)
        return jnp.concatenate([total[n, pl.ds(first, 16, stride=step), :] for n in range(3)], axis=1)

    def strided(ref, first):
        return jnp.concatenate([ref[n, pl.ds(first, 12, stride=16), :] for n in range(3)], axis=1)

    def copy(src, dst, number, peer):
        return pltpu.make_async_remote_copy(
            src_ref=src, dst_ref=dst, send_sem=send_sems.at[number], recv_sem=recv_sems.at[number],
            device_id=peer, device_id_type=MESH)

    core_copies = []
    for i in range(4):
        for j in range(12):
            core_send[i, j * 16:(j + 1) * 16, :] = gather(2 * i + 1 - core, j).astype(BF)
        if i == 0:
            pl.semaphore_wait(barrier, len(peers))
        c = copy(core_send.at[i], core_recv.at[i], i, {"core": 1 - core})
        c.start()
        core_copies.append(c)
    for i in range(4):
        for j in range(12):
            core_own[i, j * 16:(j + 1) * 16, :] = gather(2 * i + core, j)
    for i in range(4):
        core_copies[i].wait()
        core_own[i] = core_own[i] + core_recv[i].astype(F32)
    y_copies = []
    for k in range(1, 4):
        t = lax.rem(y + k, 4)
        y_send[k - 1] = core_own[t].astype(BF)
        c = copy(y_send.at[k - 1], y_recv.at[k - 1], 3 + k, {"y": t})
        c.start()
        y_copies.append(c)
    for k in range(3):
        y_copies[k].wait()
    mine = core_own[y] + y_recv[0].astype(F32) + y_recv[1].astype(F32) + y_recv[2].astype(F32)
    for n in range(3):
        y_own[n] = mine[:, n * 128:(n + 1) * 128]
    lat_send[...] = jnp.zeros_like(lat_send)
    for t in range(16):
        lat_send[t, 0:12, :] = strided(y_own, t).astype(BF)
    lat_copies = []
    for k in range(1, 16):
        t, peer = lat_peer(k)
        c = copy(lat_send.at[t], lat_recv.at[k - 1], 6 + k, peer)
        c.start()
        lat_copies.append(c)
    own = strided(y_own, lat)
    for k in range(15):
        lat_copies[k].wait()
        own = own + lat_recv[k, 0:12, :].astype(F32)
    dp_send[...] = jnp.zeros_like(dp_send)
    dp_send[0:12, :] = own
    c = copy(dp_send, dp_recv, 22, {"dp": 1 - dp})
    c.start()
    c.wait()
    out[...] = dp_send[...] + dp_recv[...]


def reduce_call(gqa, gqb, gpa, gpb):
    V = pl.BlockSpec(memory_space=pltpu.VMEM)
    return pl.pallas_call(
        reduce_kernel,
        out_shape=jax.ShapeDtypeStruct((16, D), F32),
        in_specs=[V] * 4,
        out_specs=V,
        scratch_shapes=[
            pltpu.VMEM((3, 1536, 128), F32),
            pltpu.VMEM((4, 192, D), BF),
            pltpu.VMEM((4, 192, D), BF),
            pltpu.VMEM((4, 192, D), F32),
            pltpu.VMEM((3, 192, D), BF),
            pltpu.VMEM((3, 192, D), BF),
            pltpu.VMEM((3, 192, 128), F32),
            pltpu.VMEM((16, 16, D), BF),
            pltpu.VMEM((15, 16, D), BF),
            pltpu.VMEM((16, D), F32),
            pltpu.VMEM((16, D), F32),
            pltpu.SemaphoreType.DMA((23,)),
            pltpu.SemaphoreType.DMA((23,)),
        ],
        compiler_params=pltpu.CompilerParams(
            vmem_limit_bytes=40 * 1024 * 1024, collective_id=0, has_side_effects=True),
        name="reduce_grads",
    )(gqa, gqb, gpa, gpb)


LAT = ("xl", "z")
LON = ("y", "core")
BOTH = LAT + LON


def moved(value, lat_by, lon_by, wrap):
    pairs = []
    for r in range(16):
        for c in range(8):
            if not wrap and not 0 <= r + lat_by < 16:
                continue
            pairs.append((r * 8 + c, (r + lat_by) % 16 * 8 + (c + lon_by) % 8))
    return lax.ppermute(value, BOTH, pairs)


def padded(value, to):
    return jnp.pad(value, ((0, 0), (0, 0), (0, to - value.shape[2]), (0, 0)))


def rows_of(value):
    return value.reshape(2, KC, D)


def per_device(hidden_in, grad_out, norm_gain, w_qkv, w_proj):
    r = lax.axis_index(LAT)
    both = jnp.concatenate([hidden_in, grad_out], axis=0)
    top, bottom = both[:, :15], both[:, 15:]
    a_in = moved(top[:, :, 15:45], -1, 0, False)
    b_br = moved(bottom[:, :, 45:], 1, 0, True)
    b_tl = moved(top[:, :, :15], 0, -1, True)
    b_bl = moved(bottom[:, :, :15], 1, -1, True)

    scale = jnp.where(jnp.arange(3 * D) < D, 0.125, 1.0).astype(F32)
    wqkv = (w_qkv.astype(F32) * scale).astype(BF)
    wqkv_t = wqkv.T
    gain = norm_gain.reshape(1, D)

    win_a = padded(jnp.concatenate([bottom[:, :, 15:45], a_in], axis=1), 32).reshape(2, KC, D)
    flag_a = (r < 15).astype(jnp.int32).reshape(1)
    inside = (r > 0).astype(jnp.int32).reshape(1)
    lower = jnp.concatenate([padded(b_br, 16), padded(b_bl, 16)], axis=2)
    upper = jnp.concatenate([padded(top[:, :, 45:], 16), padded(b_tl, 16)], axis=2)
    upper = jnp.where(r > 0, upper, jnp.zeros_like(upper))
    win_b = jnp.concatenate([lower, upper], axis=1).reshape(2, KC, D)
    win_a = jnp.pad(win_a, ((0, 0), (0, QC - KC), (0, 0)))
    win_b = jnp.pad(win_b, ((0, 0), (0, QC - KC), (0, 0)))

    da, gqa, gpa = window_call(32, flag_a, win_a[0], win_a[1], gain, wqkv, wqkv_t, w_proj)
    db, gqb, gpb = window_call(16, inside, win_b[0], win_b[1], gain, wqkv, wqkv_t, w_proj)

    da = da[:KC].reshape(1, 30, 32, D)
    db = db[:KC].reshape(1, 30, 32, D)
    t_m = moved(da[:, 15:, :30], 1, 0, False)
    b_r = moved(db[:, :15, :15], -1, 0, True)
    t_l = moved(db[:, 15:, 16:31], 0, 1, True)
    b_l = moved(db[:, :15, 16:31], -1, 1, True)
    back = jnp.concatenate([
        jnp.concatenate([t_l, t_m, db[:, 15:, :15]], axis=2),
        jnp.concatenate([b_l, da[:, :15, :30], b_r], axis=2)], axis=1)
    grad_in = (grad_out.astype(F32) + back.astype(F32)).astype(BF)

    sums = reduce_call(gqa, gqb, gpa, gpb)
    mine = lax.dynamic_slice_in_dim(sums, lax.axis_index("dp") * 192, 192, axis=1)[:12].T
    first = lax.axis_index(BOTH) * 9
    factor = 460800.0 ** -0.5
    column = jnp.where(first + jnp.arange(9) < D, 0.125 * factor, factor)
    return grad_in, mine[:, :9] * column[None, :], mine[:, 9:] * factor


def solution(mesh):
    split = Mesh(mesh.devices.reshape(2, 2, 8, 4, 2), ("dp", "xl", "z", "y", "core"))
    return jax.shard_map(
        per_device,
        mesh=split,
        in_specs=(P("dp", LAT, LON, None), P("dp", LAT, LON, None), P(), P(), P()),
        out_specs=(P("dp", LAT, LON, None), P("dp", BOTH), P("dp", BOTH)),
        check_vma=False,
    )
```

```python
import jax
import jax.numpy as jnp
from jax import lax
from jax.experimental import pallas as pl
from jax.experimental.pallas import tpu as pltpu
from jax.sharding import Mesh
from jax.sharding import PartitionSpec as P

HEADS = 6
D = 384
EPS = 1e-5
KC = 960
QC = 1024
CK = 480
BF = jnp.bfloat16
F32 = jnp.float32
MESH = pl.DeviceIdType.MESH
NN = (((1,), (0,)), ((), ()))
NT = (((1,), (1,)), ((), ()))
LAT = ("xl", "z")
LON = ("y", "core")
BOTH = LAT + LON


def dot(a, b, dims=NN):
    return lax.dot_general(a, b, dims, preferred_element_type=F32)


def kernel(x_ref, g_ref, gain_ref, w_ref, wp_ref, out_ref, sums_ref,
           buf, s_a, s_br, s_tl, s_bl, dbuf, ret_tm, ret_br, ret_bl, ret_tl,
           w_t, normed, rstd_s, nl, gs, q_aug, b_aug, k_aug, v_aug, qkv_t, p32, p_low, ds_low, dqkv_t, att_t,
           gp, total, core_send, core_recv, core_own, y_send, y_recv, y_own, lat_send, lat_recv,
           dp_send, dp_recv, send_sems, recv_sems):
    dp, xl, z, y, core = (lax.axis_index(n) for n in ("dp", "xl", "z", "y", "core"))
    lat = xl * 8 + z
    lon = y * 2 + core

    def at(lat_by, lon_by):
        t = lax.rem(lat + lat_by + 16, 16)
        u = lax.rem(lon + lon_by + 8, 8)
        return {"xl": t // 8, "z": lax.rem(t, 8), "y": u // 2, "core": lax.rem(u, 2)}

    def copy(src, dst, number, peer):
        return pltpu.make_async_remote_copy(
            src_ref=src, dst_ref=dst, send_sem=send_sems.at[number], recv_sem=recv_sems.at[number],
            device_id=peer, device_id_type=MESH)

    barrier = pltpu.get_barrier_semaphore()
    partner = {"core": 1 - core}
    peers = [partner, {"dp": 1 - dp}, at(0, -1), at(0, 1), at(1, -1), at(-1, 1)]
    peers += [{"y": lax.rem(y + k, 4)} for k in range(1, 4)]
    peers += [at(k, 0) for k in range(1, 16)]
    for peer in peers:
        pl.semaphore_signal(barrier, inc=1, device_id=peer, device_id_type=MESH)

    halo_a = copy(s_a, buf.at[0, :, 15:30], 23, at(-1, 0))
    halo_br = copy(s_br, buf.at[1, :, 0:15, 0:16], 24, at(1, 0))
    halo_tl = copy(s_tl, buf.at[1, :, 15:30, 16:32], 25, at(0, -1))
    halo_bl = copy(s_bl, buf.at[1, :, 0:15, 16:32], 26, at(1, -1))
    back_tm = copy(dbuf.at[0, 15:30], ret_tm, 27, at(1, 0))
    back_br = copy(dbuf.at[1, 0:15, 0:16], ret_br, 28, at(-1, 0))
    back_bl = copy(dbuf.at[1, 0:15, 16:32], ret_bl, 29, at(-1, 1))
    back_tl = copy(dbuf.at[1, 15:30, 16:32], ret_tl, 30, at(0, 1))

    pad1 = jnp.zeros((1, D), BF)
    pad2 = jnp.zeros((2, D), BF)
    for n, ref in ((0, x_ref), (1, g_ref)):
        for i in range(15):
            s_a[n, i, 0:30, :] = ref[0, i, 15:45, :]
            s_a[n, i, 30:32, :] = pad2
            s_tl[n, i, 0:15, :] = ref[0, i, 0:15, :]
            s_tl[n, i, 15:16, :] = pad1
            s_br[n, i, 0:15, :] = ref[0, 15 + i, 45:60, :]
            s_br[n, i, 15:16, :] = pad1
            s_bl[n, i, 0:15, :] = ref[0, 15 + i, 0:15, :]
            s_bl[n, i, 15:16, :] = pad1
    pl.semaphore_wait(barrier, len(peers))

    @pl.when(core == 0)
    def _():
        halo_a.start()
        halo_tl.start()
        halo_bl.start()

    @pl.when(core == 1)
    def _():
        halo_br.start()

    for n, ref in ((0, x_ref), (1, g_ref)):
        for i in range(15):
            buf[0, n, i, 0:30, :] = ref[0, 15 + i, 15:45, :]
            buf[0, n, i, 30:32, :] = pad2
            buf[1, n, 15 + i, 0:15, :] = ref[0, i, 45:60, :]
            buf[1, n, 15 + i, 15:16, :] = pad1

    gain = gain_ref[...].reshape(1, D)
    for n in range(9):
        w_t[n * 128:(n + 1) * 128, :] = w_ref[:, n * 128:(n + 1) * 128].T
    gp[...] = jnp.zeros_like(gp)
    for n in range(3):
        total[n, 0:1152, :] = jnp.zeros((1152, 128), F32)
    nl[KC:, :] = jnp.zeros((QC - KC, D), BF)
    gs[KC:, :] = jnp.zeros((QC - KC, D), BF)
    dqkv_t[:, :, KC:] = jnp.zeros((18, 64, QC - KC), BF)
    half = jnp.zeros((64, QC), BF)
    one = (lax.broadcasted_iota(jnp.int32, (128, QC), 0) == 0).astype(F32).astype(BF)
    rest = jnp.zeros((128, QC), BF)
    for h in range(HEADS):
        o = (h % 2) * 64
        q_aug[h, 64 - o:128 - o, :] = half
        b_aug[h, 64 - o:128 - o, :] = half
        q_aug[h, 128:256, :] = one
        b_aug[h, 128:256, :] = rest
    row = lax.broadcasted_iota(jnp.int32, (KC, 128), 0)
    lane = lax.broadcasted_iota(jnp.int32, (KC, 128), 1)
    ones = jnp.where(lane < 2, 1.0, 0.0).astype(BF)
    for j in range(3):
        v_aug[j, :, 128:256] = ones

    def head(h, carry):
        j = h // 2
        o = pl.multiple_of(lax.rem(h, 2) * 64, 64)
        acc = jnp.zeros((8, QC), F32)
        for k in range(0, KC, CK):
            e = jnp.exp(dot(k_aug[j, k:k + CK, :], q_aug[h]))
            p32[k:k + CK, :] = e
            acc = acc + jnp.sum(e.reshape(CK // 8, 8, QC), axis=0)
        r = 1.0 / jnp.sum(acc, axis=0, keepdims=True)
        for k in range(0, KC, CK):
            p = p32[k:k + CK, :] * r
            p32[k:k + CK, :] = p
            p_low[k:k + CK, :] = p.astype(BF)
        a = dot(qkv_t[12 + h][:, 0:KC], p_low[...])
        att_t[h] = a.astype(BF)
        less = -jnp.sum(a * b_aug[h, pl.ds(o, 64), :].astype(F32), axis=0, keepdims=True)
        high = less.astype(BF).astype(F32)
        r16 = lax.broadcasted_iota(jnp.int32, (16, QC), 0)
        b_aug[h, 128:144, :] = jnp.where(r16 == 0, high, jnp.where(r16 == 1, less - high, 0.0)).astype(BF)
        for k in range(0, KC, CK):
            dprobs = dot(v_aug[j, k:k + CK, :], b_aug[h])
            ds_low[k:k + CK, :] = (p32[k:k + CK, :] * dprobs).astype(BF)
        dqkv_t[h] = (dot(qkv_t[6 + h][:, 0:KC], ds_low[...]) * 0.125).astype(BF)
        dqkv_t[6 + h, :, 0:KC] = dot(qkv_t[h], ds_low[...], NT).astype(BF)
        dqkv_t[12 + h, :, 0:KC] = dot(b_aug[h, pl.ds(o, 64), :], p_low[...], NT).astype(BF)
        return carry

    def arrive(kind):
        @pl.when(kind == 0)
        def _():
            halo_a.wait_recv()

        @pl.when(kind == 1)
        def _():
            halo_br.wait_recv()
            halo_tl.wait_recv()
            halo_bl.wait_recv()

    def finish(kind):
        for t in range(4):
            n = 256 if t < 3 else 192
            rows = slice(t * 256, t * 256 + 256)
            dn = dot(w_ref[...], dqkv_t[:, :, rows].reshape(3 * D, 256)).T[0:n] * gain
            own = slice(t * 256, t * 256 + n)
            norm = normed[own, :]
            m1 = jnp.sum(dn, axis=1, keepdims=True) * (1 / D)
            m2 = jnp.sum(dn * norm, axis=1, keepdims=True) * (1 / D)
            d = (rstd_s[own, 0:1] * (dn - m1 - norm * m2)).astype(BF)
            dbuf[kind, t * 8:t * 8 + n // 32] = d.reshape(n // 32, 32, D)

        @pl.when(kind == 0)
        def _():
            back_tm.start()

        @pl.when(kind == 1)
        def _():
            back_br.start()
            back_bl.start()
            back_tl.start()

    def window(i, carry):
        kind = lax.rem(core + i, 2)
        edge = jnp.where(kind == 0, lat == 15, lat == 0)
        arrive(kind)

        @pl.when((i == 0) & (core == 0))
        def _():
            halo_br.start()

        @pl.when((i == 0) & (core == 1))
        def _():
            halo_a.start()
            halo_tl.start()
            halo_bl.start()

        @pl.when(edge)
        def _():
            buf[kind, :, 15:30, :, :] = jnp.zeros((2, 15, 32, D), BF)

        def norm(n, c):
            rows = pl.ds(pl.multiple_of(n * 96, 96), 96)
            cells = pl.ds(n * 3, 3)
            x = buf[kind, 0, cells].reshape(96, D).astype(F32)
            gs[rows, :] = buf[kind, 1, cells].reshape(96, D)
            centred = x - jnp.sum(x, axis=1, keepdims=True) * (1 / D)
            rstd = lax.rsqrt(jnp.sum(centred * centred, axis=1, keepdims=True) * (1 / D) + EPS)
            v = centred * rstd
            normed[rows, :] = v
            rstd_s[rows, :] = jnp.broadcast_to(rstd, (96, 128))
            nl[rows, :] = (v * gain).astype(BF)
            return c

        lax.fori_loop(0, KC // 96, norm, 0)
        q = (dot(w_t[0:D, :], nl[...], NT).astype(BF).astype(F32) * 0.125).astype(BF)
        qkv_t[0:6] = q.reshape(6, 64, QC)
        for part in (1, 2):
            rows = slice(part * D, (part + 1) * D)
            qkv_t[part * 6:part * 6 + 6] = dot(w_t[rows, :], nl[...], NT).astype(BF).reshape(6, 64, QC)
        bt = dot(wp_ref[...], gs[...], NT).astype(BF).reshape(6, 64, QC)
        for h in range(HEADS):
            o = (h % 2) * 64
            q_aug[h, o:o + 64, :] = qkv_t[h]
            b_aug[h, o:o + 64, :] = bt[h]
        slot = jnp.where(kind == 0, row & 31, (row & 15) + 15)
        bad = (slot >= 30) | ((row >= KC // 2) & edge)
        bias = jnp.where((lane == 0) & bad, -30000.0, 0.0).astype(BF)
        for j in range(3):
            cols = slice(D + j * 128, D + (j + 1) * 128)
            k_aug[j, :, 0:128] = dot(nl[0:KC, :], w_ref[:, cols]).astype(BF)
            cols = slice(2 * D + j * 128, 2 * D + (j + 1) * 128)
            v_aug[j, :, 0:128] = dot(nl[0:KC, :], w_ref[:, cols]).astype(BF)
            k_aug[j, :, 128:256] = bias
        lax.fori_loop(0, HEADS, head, 0)
        dw = dot(dqkv_t[...].reshape(3 * D, QC), nl[...])
        for n in range(3):
            total[n, 0:1152, :] += dw[:, n * 128:(n + 1) * 128]
        gp[...] += dot(att_t[...].reshape(D, QC), gs[...])

        @pl.when(i == 0)
        def _():
            finish(kind)

        return carry

    lax.fori_loop(0, 2, window, 0)

    for n in range(3):
        total[n, 1152:1536, :] = gp[n * 128:(n + 1) * 128, :].T

    def gather(at_lon, j):
        first, step = (9 * at_lon + j, 72) if j < 9 else (1152 + 3 * at_lon + j - 9, 24)
        return jnp.concatenate([total[n, pl.ds(first, 16, stride=step), :] for n in range(3)], axis=1)

    core_copies = [copy(core_send.at[i], core_recv.at[i], i, partner) for i in range(4)]
    for i in range(4):
        for j in range(12):
            core_send[i, j * 16:(j + 1) * 16, :] = gather(2 * i + 1 - core, j).astype(BF)
        core_copies[i].start()
    for i in range(4):
        for j in range(12):
            core_own[i, j * 16:(j + 1) * 16, :] = gather(2 * i + core, j)
    finish(1 - core)
    for i in range(4):
        core_copies[i].wait()
        core_own[i] = core_own[i] + core_recv[i].astype(F32)
    y_copies = []
    for k in range(1, 4):
        t = lax.rem(y + k, 4)
        y_send[k - 1] = core_own[t].astype(BF)
        c = copy(y_send.at[k - 1], y_recv.at[k - 1], 3 + k, {"y": t})
        c.start()
        y_copies.append(c)
    back_tm.wait_recv()
    back_br.wait_recv()
    back_bl.wait_recv()
    back_tl.wait_recv()
    for i in range(15):
        for r, c0, c1, part in (
                (i, 0, 15, ret_tl[i, 0:15, :]), (i, 15, 45, ret_tm[i, 0:30, :]),
                (i, 45, 60, dbuf[1, 15 + i, 0:15, :]), (15 + i, 0, 15, ret_bl[i, 0:15, :]),
                (15 + i, 15, 45, dbuf[0, i, 0:30, :]), (15 + i, 45, 60, ret_br[i, 0:15, :])):
            out_ref[0, r, c0:c1, :] = (g_ref[0, r, c0:c1, :].astype(F32) + part.astype(F32)).astype(BF)
    for k in range(3):
        y_copies[k].wait()
    mine = core_own[y] + y_recv[0].astype(F32) + y_recv[1].astype(F32) + y_recv[2].astype(F32)
    for n in range(3):
        y_own[n] = mine[:, n * 128:(n + 1) * 128]

    def strided(first):
        return jnp.concatenate([y_own[n, pl.ds(first, 12, stride=16), :] for n in range(3)], axis=1)

    spare = jnp.zeros((4, D), F32)
    for t in range(16):
        lat_send[t] = jnp.concatenate([strided(t), spare], axis=0).astype(BF)
    lat_copies = []
    for k in range(1, 16):
        c = copy(lat_send.at[lax.rem(lat + k, 16)], lat_recv.at[k - 1], 6 + k, at(k, 0))
        c.start()
        lat_copies.append(c)
    own = strided(lat)
    for k in range(15):
        lat_copies[k].wait()
        own = own + lat_recv[k, 0:12, :].astype(F32)
    dp_send[...] = jnp.concatenate([own, spare], axis=0)
    c = copy(dp_send, dp_recv, 22, {"dp": 1 - dp})
    c.start()
    c.wait()
    sums_ref[...] = dp_send[...] + dp_recv[...]
    for c in (halo_a, halo_br, halo_tl, halo_bl, back_tm, back_br, back_bl, back_tl):
        c.wait_send()


def per_device(hidden_in, grad_out, norm_gain, w_qkv, w_proj):
    V = pl.BlockSpec(memory_space=pltpu.VMEM)
    scratch = [
        ((2, 2, 30, 32, D), BF), ((2, 15, 32, D), BF), ((2, 15, 16, D), BF), ((2, 15, 16, D), BF),
        ((2, 15, 16, D), BF), ((2, 30, 32, D), BF), ((15, 32, D), BF), ((15, 16, D), BF), ((15, 16, D), BF),
        ((15, 16, D), BF),
        ((3 * D, D), BF), ((KC, D), F32), ((KC, 128), F32), ((QC, D), BF), ((QC, D), BF), ((6, 256, QC), BF),
        ((6, 256, QC), BF), ((3, KC, 256), BF), ((3, KC, 256), BF), ((18, 64, QC), BF), ((KC, QC), F32),
        ((KC, QC), BF), ((KC, QC), BF), ((18, 64, QC), BF), ((6, 64, QC), BF),
        ((D, D), F32), ((3, 1536, 128), F32), ((4, 192, D), BF), ((4, 192, D), BF), ((4, 192, D), F32),
        ((3, 192, D), BF), ((3, 192, D), BF), ((3, 192, 128), F32), ((16, 16, D), BF), ((15, 16, D), BF),
        ((16, D), F32), ((16, D), F32),
    ]
    grad_in, sums = pl.pallas_call(
        kernel,
        out_shape=(jax.ShapeDtypeStruct(grad_out.shape, BF), jax.ShapeDtypeStruct((16, D), F32)),
        in_specs=[V] * 5,
        out_specs=(V, V),
        scratch_shapes=[pltpu.VMEM(s, d) for s, d in scratch] + [pltpu.SemaphoreType.DMA((31,))] * 2,
        compiler_params=pltpu.CompilerParams(
            vmem_limit_bytes=63 * 1024 * 1024, collective_id=0, has_side_effects=True),
        name="block_backward",
    )(hidden_in, grad_out, norm_gain, w_qkv, w_proj)
    mine = lax.dynamic_slice_in_dim(sums, lax.axis_index("dp") * 192, 192, axis=1)[:12].T
    factor = 460800.0 ** -0.5
    return grad_in, mine[:, :9] * factor, mine[:, 9:] * factor


def solution(mesh):
    split = Mesh(mesh.devices.reshape(2, 2, 8, 4, 2), ("dp", "xl", "z", "y", "core"))
    return jax.shard_map(
        per_device,
        mesh=split,
        in_specs=(P("dp", LAT, LON, None), P("dp", LAT, LON, None), P(), P(), P()),
        out_specs=(P("dp", LAT, LON, None), P("dp", BOTH), P("dp", BOTH)),
        check_vma=False,
    )
```

```python
import jax
import jax.numpy as jnp
from jax import lax
from jax.experimental import pallas as pl
from jax.experimental.pallas import tpu as pltpu
from jax.sharding import Mesh
from jax.sharding import PartitionSpec as P

HEADS = 6
D = 384
EPS = 1e-5
KC = 960
QC = 1024
CK = 480
BF = jnp.bfloat16
F32 = jnp.float32
MESH = pl.DeviceIdType.MESH
NN = (((1,), (0,)), ((), ()))
NT = (((1,), (1,)), ((), ()))
LAT = ("xl", "z")
LON = ("y", "core")
BOTH = LAT + LON


def dot(a, b, dims=NN):
    return lax.dot_general(a, b, dims, preferred_element_type=F32)


def kernel(x_hbm, g_hbm, gain_ref, w_ref, wp_ref, out_ref, qkv_ref, proj_ref,
           x_ref, g_ref,
           buf, s_a, s_br, s_tl, s_bl, dbuf, ret_tm, ret_br, ret_bl, ret_tl,
           w_t, normed, rstd_s, nl, gs, q_aug, b_aug, k_aug, v_aug, qkv_t, p32, p_low, ds_low, dqkv_t, att_t,
           gp, total, core_send, core_recv, core_own, y_send, y_recv, y_own, lat_send, lat_recv,
           dp_send, dp_recv, send_sems, recv_sems, load_sems):
    dp, xl, z, y, core = (lax.axis_index(n) for n in ("dp", "xl", "z", "y", "core"))
    loads = [pltpu.make_async_copy(src, dst, load_sems.at[n]) for n, (src, dst) in enumerate((
        (x_hbm.at[0], x_ref), (g_hbm.at[0], g_ref)))]
    for load in loads:
        load.start()
    lat = xl * 8 + z
    lon = y * 2 + core

    def at(lat_by, lon_by):
        t = lax.rem(lat + lat_by + 16, 16)
        u = lax.rem(lon + lon_by + 8, 8)
        return {"xl": t // 8, "z": lax.rem(t, 8), "y": u // 2, "core": lax.rem(u, 2)}

    def copy(src, dst, number, peer):
        return pltpu.make_async_remote_copy(
            src_ref=src, dst_ref=dst, send_sem=send_sems.at[number], recv_sem=recv_sems.at[number],
            device_id=peer, device_id_type=MESH)

    barrier = pltpu.get_barrier_semaphore()
    partner = {"core": 1 - core}
    peers = [partner, {"dp": 1 - dp}, at(0, -1), at(0, 1), at(1, -1), at(-1, 1)]
    peers += [{"y": lax.rem(y + k, 4)} for k in range(1, 4)]
    peers += [at(k, 0) for k in range(1, 16)]
    for peer in peers:
        pl.semaphore_signal(barrier, inc=1, device_id=peer, device_id_type=MESH)

    halo_a = [copy(s_a.at[n], buf.at[0, n, 15:30], 26 + n, at(-1, 0)) for n in range(2)]
    halo_br = [copy(s_br.at[n], buf.at[1, n, 0:15, 0:16], 28 + n, at(1, 0)) for n in range(2)]
    halo_tl = [copy(s_tl.at[n], buf.at[1, n, 15:30, 16:32], 30 + n, at(0, -1)) for n in range(2)]
    halo_bl = [copy(s_bl.at[n], buf.at[1, n, 0:15, 16:32], 32 + n, at(1, -1)) for n in range(2)]
    back_tm = copy(dbuf.at[0, 15:30], ret_tm, 34, at(1, 0))
    back_br = copy(dbuf.at[1, 0:15, 0:16], ret_br, 35, at(-1, 0))
    back_bl = copy(dbuf.at[1, 0:15, 16:32], ret_bl, 36, at(-1, 1))
    back_tl = copy(dbuf.at[1, 15:30, 16:32], ret_tl, 37, at(0, 1))

    pad1 = jnp.zeros((1, D), BF)
    pad2 = jnp.zeros((2, D), BF)
    for n, ref in ((0, x_ref), (1, g_ref)):
        loads[n].wait()
        for i in range(15):
            s_a[n, i, 0:30, :] = ref[i, 15:45, :]
            s_a[n, i, 30:32, :] = pad2
            s_tl[n, i, 0:15, :] = ref[i, 0:15, :]
            s_tl[n, i, 15:16, :] = pad1
            s_br[n, i, 0:15, :] = ref[15 + i, 45:60, :]
            s_br[n, i, 15:16, :] = pad1
            s_bl[n, i, 0:15, :] = ref[15 + i, 0:15, :]
            s_bl[n, i, 15:16, :] = pad1
        if n == 0:
            pl.semaphore_wait(barrier, len(peers))

        @pl.when(core == 0)
        def _():
            halo_a[n].start()
            halo_tl[n].start()
            halo_bl[n].start()

        @pl.when(core == 1)
        def _():
            halo_br[n].start()

    for n, ref in ((0, x_ref), (1, g_ref)):
        for i in range(15):
            buf[0, n, i, 0:30, :] = ref[15 + i, 15:45, :]
            buf[0, n, i, 30:32, :] = pad2
            buf[1, n, 15 + i, 0:15, :] = ref[i, 45:60, :]
            buf[1, n, 15 + i, 15:16, :] = pad1

    gain = gain_ref[...].reshape(1, D)
    for n in range(9):
        w_t[n * 128:(n + 1) * 128, :] = w_ref[:, n * 128:(n + 1) * 128].T
    gp[...] = jnp.zeros_like(gp)
    for n in range(3):
        total[n, 0:1152, :] = jnp.zeros((1152, 128), F32)
    nl[KC:, :] = jnp.zeros((QC - KC, D), BF)
    gs[KC:, :] = jnp.zeros((QC - KC, D), BF)
    dqkv_t[:, :, KC:] = jnp.zeros((18, 64, QC - KC), BF)
    half = jnp.zeros((64, QC), BF)
    one = (lax.broadcasted_iota(jnp.int32, (128, QC), 0) == 0).astype(F32).astype(BF)
    rest = jnp.zeros((128, QC), BF)
    for h in range(HEADS):
        o = (h % 2) * 64
        q_aug[h, 64 - o:128 - o, :] = half
        b_aug[h, 64 - o:128 - o, :] = half
        q_aug[h, 128:256, :] = one
        b_aug[h, 128:256, :] = rest
    row = lax.broadcasted_iota(jnp.int32, (KC, 128), 0)
    lane = lax.broadcasted_iota(jnp.int32, (KC, 128), 1)
    ones = jnp.where(lane < 2, 1.0, 0.0).astype(BF)
    for j in range(3):
        v_aug[j, :, 128:256] = ones

    def head(h, carry):
        j = h // 2
        o = pl.multiple_of(lax.rem(h, 2) * 64, 64)
        acc = jnp.zeros((8, QC), F32)
        for k in range(0, KC, CK):
            e = jnp.exp(dot(k_aug[j, k:k + CK, :], q_aug[h]))
            p32[k:k + CK, :] = e
            acc = acc + jnp.sum(e.reshape(CK // 8, 8, QC), axis=0)
        r = 1.0 / jnp.sum(acc, axis=0, keepdims=True)
        for k in range(0, KC, CK):
            p = p32[k:k + CK, :] * r
            p32[k:k + CK, :] = p
            p_low[k:k + CK, :] = p.astype(BF)
        a = dot(qkv_t[12 + h][:, 0:KC], p_low[...])
        att_t[h] = a.astype(BF)
        less = -jnp.sum(a * b_aug[h, pl.ds(o, 64), :].astype(F32), axis=0, keepdims=True)
        high = less.astype(BF).astype(F32)
        r16 = lax.broadcasted_iota(jnp.int32, (16, QC), 0)
        b_aug[h, 128:144, :] = jnp.where(r16 == 0, high, jnp.where(r16 == 1, less - high, 0.0)).astype(BF)
        for k in range(0, KC, CK):
            dprobs = dot(v_aug[j, k:k + CK, :], b_aug[h])
            ds_low[k:k + CK, :] = (p32[k:k + CK, :] * dprobs).astype(BF)
        dqkv_t[h] = (dot(qkv_t[6 + h][:, 0:KC], ds_low[...]) * 0.125).astype(BF)
        dqkv_t[6 + h, :, 0:KC] = dot(qkv_t[h], ds_low[...], NT).astype(BF)
        dqkv_t[12 + h, :, 0:KC] = dot(b_aug[h, pl.ds(o, 64), :], p_low[...], NT).astype(BF)
        return carry

    def arrive(kind, n):
        @pl.when(kind == 0)
        def _():
            halo_a[n].wait_recv()

        @pl.when(kind == 1)
        def _():
            halo_br[n].wait_recv()
            halo_tl[n].wait_recv()
            halo_bl[n].wait_recv()

    def clear(kind, n, edge):
        @pl.when(edge)
        def _():
            buf[kind, n, 15:30, :, :] = jnp.zeros((15, 32, D), BF)

    def finish(kind):
        for t in range(4):
            n = 256 if t < 3 else 192
            rows = slice(t * 256, t * 256 + 256)
            dn = dot(w_ref[...], dqkv_t[:, :, rows].reshape(3 * D, 256)).T[0:n] * gain
            own = slice(t * 256, t * 256 + n)
            norm = normed[own, :]
            m1 = jnp.sum(dn, axis=1, keepdims=True) * (1 / D)
            m2 = jnp.sum(dn * norm, axis=1, keepdims=True) * (1 / D)
            d = (rstd_s[own, 0:1] * (dn - m1 - norm * m2)).astype(BF)
            dbuf[kind, t * 8:t * 8 + n // 32] = d.reshape(n // 32, 32, D)

        @pl.when(kind == 0)
        def _():
            back_tm.start()

        @pl.when(kind == 1)
        def _():
            back_br.start()
            back_bl.start()
            back_tl.start()

    def window(i, carry):
        kind = lax.rem(core + i, 2)
        edge = jnp.where(kind == 0, lat == 15, lat == 0)
        arrive(kind, 0)
        clear(kind, 0, edge)

        def norm(n, c):
            rows = pl.ds(pl.multiple_of(n * 96, 96), 96)
            cells = pl.ds(n * 3, 3)
            x = buf[kind, 0, cells].reshape(96, D).astype(F32)
            centred = x - jnp.sum(x, axis=1, keepdims=True) * (1 / D)
            rstd = lax.rsqrt(jnp.sum(centred * centred, axis=1, keepdims=True) * (1 / D) + EPS)
            v = centred * rstd
            normed[rows, :] = v
            rstd_s[rows, :] = jnp.broadcast_to(rstd, (96, 128))
            nl[rows, :] = (v * gain).astype(BF)
            return c

        lax.fori_loop(0, KC // 96, norm, 0)
        q = (dot(w_t[0:D, :], nl[...], NT).astype(BF).astype(F32) * 0.125).astype(BF)
        qkv_t[0:6] = q.reshape(6, 64, QC)
        for part in (1, 2):
            rows = slice(part * D, (part + 1) * D)
            qkv_t[part * 6:part * 6 + 6] = dot(w_t[rows, :], nl[...], NT).astype(BF).reshape(6, 64, QC)
        arrive(kind, 1)
        clear(kind, 1, edge)

        @pl.when((i == 0) & (core == 0))
        def _():
            for n in range(2):
                halo_br[n].start()

        @pl.when((i == 0) & (core == 1))
        def _():
            for n in range(2):
                halo_a[n].start()
                halo_tl[n].start()
                halo_bl[n].start()

        gs[0:KC, :] = buf[kind, 1].reshape(KC, D)
        bt = dot(wp_ref[...], gs[...], NT).astype(BF).reshape(6, 64, QC)
        for h in range(HEADS):
            o = (h % 2) * 64
            q_aug[h, o:o + 64, :] = qkv_t[h]
            b_aug[h, o:o + 64, :] = bt[h]
        slot = jnp.where(kind == 0, row & 31, (row & 15) + 15)
        bad = (slot >= 30) | ((row >= KC // 2) & edge)
        bias = jnp.where((lane == 0) & bad, -30000.0, 0.0).astype(BF)
        for j in range(3):
            cols = slice(D + j * 128, D + (j + 1) * 128)
            k_aug[j, :, 0:128] = dot(nl[0:KC, :], w_ref[:, cols]).astype(BF)
            cols = slice(2 * D + j * 128, 2 * D + (j + 1) * 128)
            v_aug[j, :, 0:128] = dot(nl[0:KC, :], w_ref[:, cols]).astype(BF)
            k_aug[j, :, 128:256] = bias
        lax.fori_loop(0, HEADS, head, 0)
        dw = dot(dqkv_t[...].reshape(3 * D, QC), nl[...])
        for n in range(3):
            total[n, 0:1152, :] += dw[:, n * 128:(n + 1) * 128]
        gp[...] += dot(att_t[...].reshape(D, QC), gs[...])

        @pl.when(i == 0)
        def _():
            finish(kind)

        return carry

    lax.fori_loop(0, 2, window, 0)

    for n in range(3):
        total[n, 1152:1536, :] = gp[n * 128:(n + 1) * 128, :].T

    def gather(at_lon, j):
        first, step = (9 * at_lon + j, 72) if j < 9 else (1152 + 3 * at_lon + j - 9, 24)
        return jnp.concatenate([total[n, pl.ds(first, 16, stride=step), :] for n in range(3)], axis=1)

    turns = [lax.rem(y + k, 4) for k in (2, 1, 3, 0)]
    core_copies = [copy(core_send.at[i], core_recv.at[i], i, partner) for i in range(4)]
    for i in range(4):
        for j in range(12):
            core_send[i, j * 16:(j + 1) * 16, :] = gather(2 * turns[i] + 1 - core, j).astype(BF)
        core_copies[i].start()
    for i in range(4):
        for j in range(12):
            core_own[i, j * 16:(j + 1) * 16, :] = gather(2 * turns[i] + core, j)
    finish(1 - core)
    up, down = {"y": turns[1]}, {"y": turns[2]}
    y_copies = [copy(y_send.at[n], y_recv.at[n], 4 + n, (up, down)[n % 2]) for n in range(6)]
    first, second = slice(0, 96), slice(96, 192)

    def send_y(n, value):
        y_send[n] = value.astype(BF)
        y_copies[n].start()

    for i in range(4):
        core_copies[i].wait()
        core_own[i] = core_own[i] + core_recv[i].astype(F32)
        if i == 0:
            send_y(0, core_own[0, first])
            send_y(1, core_own[0, second])
        if i == 1:
            send_y(2, core_own[1, second])
        if i == 2:
            send_y(3, core_own[2, first])
    y_copies[0].wait()
    send_y(4, core_own[1, first] + y_recv[0].astype(F32))
    y_copies[1].wait()
    send_y(5, core_own[2, second] + y_recv[1].astype(F32))
    back_tm.wait_recv()
    back_br.wait_recv()
    back_bl.wait_recv()
    back_tl.wait_recv()
    for i in range(15):
        for r, c0, c1, part in (
                (i, 0, 15, ret_tl[i, 0:15, :]), (i, 15, 45, ret_tm[i, 0:30, :]),
                (i, 45, 60, dbuf[1, 15 + i, 0:15, :]), (15 + i, 0, 15, ret_bl[i, 0:15, :]),
                (15 + i, 15, 45, dbuf[0, i, 0:30, :]), (15 + i, 45, 60, ret_br[i, 0:15, :])):
            out_ref[0, r, c0:c1, :] = (g_ref[r, c0:c1, :].astype(F32) + part.astype(F32)).astype(BF)
    for n in range(2, 6):
        y_copies[n].wait()
    low = core_own[3, first] + y_recv[4].astype(F32) + y_recv[3].astype(F32)
    high = core_own[3, second] + y_recv[2].astype(F32) + y_recv[5].astype(F32)
    for n in range(3):
        y_own[n, first] = low[:, n * 128:(n + 1) * 128]
        y_own[n, second] = high[:, n * 128:(n + 1) * 128]

    def strided(first):
        return jnp.concatenate([y_own[n, pl.ds(first, 12, stride=16), :] for n in range(3)], axis=1)

    spare = jnp.zeros((4, D), F32)
    for t in range(16):
        lat_send[t] = jnp.concatenate([strided(t), spare], axis=0).astype(BF)
    lat_copies = []
    for k in range(1, 16):
        c = copy(lat_send.at[lax.rem(lat + k, 16)], lat_recv.at[k - 1], 9 + k, at(k, 0))
        c.start()
        lat_copies.append(c)
    own = strided(lat)
    for k in range(15):
        lat_copies[k].wait()
        own = own + lat_recv[k, 0:12, :].astype(F32)
    dp_send[...] = jnp.concatenate([own, spare], axis=0)
    c = copy(dp_send, dp_recv, 25, {"dp": 1 - dp})
    c.start()
    c.wait()
    factor = 460800.0 ** -0.5
    both = (dp_send[...] + dp_recv[...]) * factor
    mine = jnp.where(dp == 0, both, pltpu.roll(both, 192, 1))
    qkv_ref[...] = mine[0:9, 0:192]
    proj_ref[...] = mine[9:12, 0:192]
    for c in (*halo_a, *halo_br, *halo_tl, *halo_bl, back_tm, back_br, back_bl, back_tl):
        c.wait_send()


def per_device(hidden_in, grad_out, norm_gain, w_qkv, w_proj):
    V = pl.BlockSpec(memory_space=pltpu.VMEM)
    scratch = [
        ((30, 60, D), BF), ((30, 60, D), BF),
        ((2, 2, 30, 32, D), BF), ((2, 15, 32, D), BF), ((2, 15, 16, D), BF), ((2, 15, 16, D), BF),
        ((2, 15, 16, D), BF), ((2, 30, 32, D), BF), ((15, 32, D), BF), ((15, 16, D), BF), ((15, 16, D), BF),
        ((15, 16, D), BF),
        ((3 * D, D), BF), ((KC, D), F32), ((KC, 128), F32), ((QC, D), BF), ((QC, D), BF), ((6, 256, QC), BF),
        ((6, 256, QC), BF), ((3, KC, 256), BF), ((3, KC, 256), BF), ((18, 64, QC), BF), ((KC, QC), F32),
        ((KC, QC), BF), ((KC, QC), BF), ((18, 64, QC), BF), ((6, 64, QC), BF),
        ((D, D), F32), ((3, 1536, 128), F32), ((4, 192, D), BF), ((4, 192, D), BF), ((4, 192, D), F32),
        ((6, 96, D), BF), ((6, 96, D), BF), ((3, 192, 128), F32), ((16, 16, D), BF), ((15, 16, D), BF),
        ((16, D), F32), ((16, D), F32),
    ]
    H = pl.BlockSpec(memory_space=pltpu.HBM)
    grad_in, qkv, proj = pl.pallas_call(
        kernel,
        out_shape=(jax.ShapeDtypeStruct(grad_out.shape, BF), jax.ShapeDtypeStruct((9, 192), F32),
                   jax.ShapeDtypeStruct((3, 192), F32)),
        in_specs=[H, H, V, V, V],
        out_specs=(V, V, V),
        scratch_shapes=[pltpu.VMEM(s, d) for s, d in scratch] + [pltpu.SemaphoreType.DMA((38,))] * 2
        + [pltpu.SemaphoreType.DMA((2,))],
        compiler_params=pltpu.CompilerParams(
            vmem_limit_bytes=50 * 1024 * 1024, collective_id=0, has_side_effects=True),
        name="block_backward",
    )(hidden_in, grad_out, norm_gain, w_qkv, w_proj)
    return grad_in, qkv.T, proj.T


def solution(mesh):
    split = Mesh(mesh.devices.reshape(2, 2, 8, 4, 2), ("dp", "xl", "z", "y", "core"))
    return jax.shard_map(
        per_device,
        mesh=split,
        in_specs=(P("dp", LAT, LON, None), P("dp", LAT, LON, None), P(), P(), P()),
        out_specs=(P("dp", LAT, LON, None), P("dp", BOTH), P("dp", BOTH)),
        check_vma=False,
    )
```

```python
import jax
import jax.numpy as jnp
from jax import lax
from jax.experimental import pallas as pl
from jax.experimental.pallas import tpu as pltpu
from jax.sharding import Mesh
from jax.sharding import PartitionSpec as P

HEADS = 6
D = 384
EPS = 1e-5
KC = 960
QC = 1024
CK = 480
BF = jnp.bfloat16
F32 = jnp.float32
MESH = pl.DeviceIdType.MESH
NN = (((1,), (0,)), ((), ()))
NT = (((1,), (1,)), ((), ()))
LAT = ("xl", "z")
LON = ("y", "core")
BOTH = LAT + LON


def dot(a, b, dims=NN):
    return lax.dot_general(a, b, dims, preferred_element_type=F32)


def kernel(x_hbm, g_hbm, gain_hbm, w_hbm, wp_hbm, out_ref, qkv_ref, proj_ref,
           x_ref, g_ref, gain_ref, w_ref, wp_ref,
           buf, s_a, s_br, s_tl, s_bl, dbuf, ret_tm, ret_br, ret_bl, ret_tl,
           w_t, normed, rstd_s, nl, gs, q_aug, b_aug, k_aug, v_aug, qkv_t, p32, p_low, ds_low, dqkv_t, att_t,
           gp, total, core_send, core_recv, core_own, y_send, y_recv, y_own, lat_send, lat_recv,
           dp_send, dp_recv, send_sems, recv_sems, load_sems):
    dp, xl, z, y, core = (lax.axis_index(n) for n in ("dp", "xl", "z", "y", "core"))
    loads = [pltpu.make_async_copy(src, dst, load_sems.at[n]) for n, (src, dst) in enumerate((
        (x_hbm.at[0], x_ref), (g_hbm.at[0], g_ref), (w_hbm, w_ref), (wp_hbm, wp_ref), (gain_hbm, gain_ref)))]
    for load in loads:
        load.start()
    lat = xl * 8 + z
    lon = y * 2 + core

    def at(lat_by, lon_by):
        t = lax.rem(lat + lat_by + 16, 16)
        u = lax.rem(lon + lon_by + 8, 8)
        return {"xl": t // 8, "z": lax.rem(t, 8), "y": u // 2, "core": lax.rem(u, 2)}

    def copy(src, dst, number, peer):
        return pltpu.make_async_remote_copy(
            src_ref=src, dst_ref=dst, send_sem=send_sems.at[number], recv_sem=recv_sems.at[number],
            device_id=peer, device_id_type=MESH)

    barrier = pltpu.get_barrier_semaphore()
    partner = {"core": 1 - core}
    peers = [partner, {"dp": 1 - dp}, at(0, -1), at(0, 1), at(1, -1), at(-1, 1)]
    peers += [{"y": lax.rem(y + k, 4)} for k in range(1, 4)]
    peers += [at(k, 0) for k in range(1, 16)]
    for peer in peers:
        pl.semaphore_signal(barrier, inc=1, device_id=peer, device_id_type=MESH)

    halo_a = [copy(s_a.at[n], buf.at[0, n, 15:30], 26 + n, at(-1, 0)) for n in range(2)]
    halo_br = [copy(s_br.at[n], buf.at[1, n, 0:15, 0:16], 28 + n, at(1, 0)) for n in range(2)]
    halo_tl = [copy(s_tl.at[n], buf.at[1, n, 15:30, 16:32], 30 + n, at(0, -1)) for n in range(2)]
    halo_bl = [copy(s_bl.at[n], buf.at[1, n, 0:15, 16:32], 32 + n, at(1, -1)) for n in range(2)]
    back_tm = copy(dbuf.at[0, 15:30], ret_tm, 34, at(1, 0))
    back_br = copy(dbuf.at[1, 0:15, 0:16], ret_br, 35, at(-1, 0))
    back_bl = copy(dbuf.at[1, 0:15, 16:32], ret_bl, 36, at(-1, 1))
    back_tl = copy(dbuf.at[1, 15:30, 16:32], ret_tl, 37, at(0, 1))

    pad1 = jnp.zeros((1, D), BF)
    pad2 = jnp.zeros((2, D), BF)
    for n, ref in ((0, x_ref), (1, g_ref)):
        loads[n].wait()
        for i in range(15):
            s_a[n, i, 0:30, :] = ref[i, 15:45, :]
            s_a[n, i, 30:32, :] = pad2
            s_tl[n, i, 0:15, :] = ref[i, 0:15, :]
            s_tl[n, i, 15:16, :] = pad1
            s_br[n, i, 0:15, :] = ref[15 + i, 45:60, :]
            s_br[n, i, 15:16, :] = pad1
            s_bl[n, i, 0:15, :] = ref[15 + i, 0:15, :]
            s_bl[n, i, 15:16, :] = pad1
        if n == 0:
            pl.semaphore_wait(barrier, len(peers))

        @pl.when(core == 0)
        def _():
            halo_a[n].start()
            halo_tl[n].start()
            halo_bl[n].start()

        @pl.when(core == 1)
        def _():
            halo_br[n].start()

    for n, ref in ((0, x_ref), (1, g_ref)):
        for i in range(15):
            buf[0, n, i, 0:30, :] = ref[15 + i, 15:45, :]
            buf[0, n, i, 30:32, :] = pad2
            buf[1, n, 15 + i, 0:15, :] = ref[i, 45:60, :]
            buf[1, n, 15 + i, 15:16, :] = pad1

    for load in loads[2:]:
        load.wait()
    gain = gain_ref[...].reshape(1, D)
    for n in range(9):
        w_t[n * 128:(n + 1) * 128, :] = w_ref[:, n * 128:(n + 1) * 128].T
    gp[...] = jnp.zeros_like(gp)
    for n in range(3):
        total[n, 0:1152, :] = jnp.zeros((1152, 128), F32)
    nl[KC:, :] = jnp.zeros((QC - KC, D), BF)
    gs[KC:, :] = jnp.zeros((QC - KC, D), BF)
    dqkv_t[:, :, KC:] = jnp.zeros((18, 64, QC - KC), BF)
    half = jnp.zeros((64, QC), BF)
    one = (lax.broadcasted_iota(jnp.int32, (128, QC), 0) == 0).astype(F32).astype(BF)
    rest = jnp.zeros((128, QC), BF)
    for h in range(HEADS):
        o = (h % 2) * 64
        q_aug[h, 64 - o:128 - o, :] = half
        b_aug[h, 64 - o:128 - o, :] = half
        q_aug[h, 128:256, :] = one
        b_aug[h, 128:256, :] = rest
    row = lax.broadcasted_iota(jnp.int32, (KC, 128), 0)
    lane = lax.broadcasted_iota(jnp.int32, (KC, 128), 1)
    ones = jnp.where(lane < 2, 1.0, 0.0).astype(BF)
    for j in range(3):
        v_aug[j, :, 128:256] = ones

    def head(h, carry):
        j = h // 2
        o = pl.multiple_of(lax.rem(h, 2) * 64, 64)
        acc = jnp.zeros((8, QC), F32)
        for k in range(0, KC, CK):
            e = jnp.exp(dot(k_aug[j, k:k + CK, :], q_aug[h]))
            p32[k:k + CK, :] = e
            acc = acc + jnp.sum(e.reshape(CK // 8, 8, QC), axis=0)
        r = 1.0 / jnp.sum(acc, axis=0, keepdims=True)
        for k in range(0, KC, CK):
            p = p32[k:k + CK, :] * r
            p32[k:k + CK, :] = p
            p_low[k:k + CK, :] = p.astype(BF)
        a = dot(qkv_t[12 + h][:, 0:KC], p_low[...])
        att_t[h] = a.astype(BF)
        less = -jnp.sum(a * b_aug[h, pl.ds(o, 64), :].astype(F32), axis=0, keepdims=True)
        high = less.astype(BF).astype(F32)
        r16 = lax.broadcasted_iota(jnp.int32, (16, QC), 0)
        b_aug[h, 128:144, :] = jnp.where(r16 == 0, high, jnp.where(r16 == 1, less - high, 0.0)).astype(BF)
        for k in range(0, KC, CK):
            dprobs = dot(v_aug[j, k:k + CK, :], b_aug[h])
            ds_low[k:k + CK, :] = (p32[k:k + CK, :] * dprobs).astype(BF)
        dqkv_t[h] = (dot(qkv_t[6 + h][:, 0:KC], ds_low[...]) * 0.125).astype(BF)
        dqkv_t[6 + h, :, 0:KC] = dot(qkv_t[h], ds_low[...], NT).astype(BF)
        dqkv_t[12 + h, :, 0:KC] = dot(b_aug[h, pl.ds(o, 64), :], p_low[...], NT).astype(BF)
        return carry

    def arrive(kind, n):
        @pl.when(kind == 0)
        def _():
            halo_a[n].wait_recv()

        @pl.when(kind == 1)
        def _():
            halo_br[n].wait_recv()
            halo_tl[n].wait_recv()
            halo_bl[n].wait_recv()

    def clear(kind, n, edge):
        @pl.when(edge)
        def _():
            buf[kind, n, 15:30, :, :] = jnp.zeros((15, 32, D), BF)

    def finish(kind):
        for t in range(4):
            n = 256 if t < 3 else 192
            rows = slice(t * 256, t * 256 + 256)
            dn = dot(w_ref[...], dqkv_t[:, :, rows].reshape(3 * D, 256)).T[0:n] * gain
            own = slice(t * 256, t * 256 + n)
            norm = normed[own, :]
            m1 = jnp.sum(dn, axis=1, keepdims=True) * (1 / D)
            m2 = jnp.sum(dn * norm, axis=1, keepdims=True) * (1 / D)
            d = (rstd_s[own, 0:1] * (dn - m1 - norm * m2)).astype(BF)
            dbuf[kind, t * 8:t * 8 + n // 32] = d.reshape(n // 32, 32, D)

        @pl.when(kind == 0)
        def _():
            back_tm.start()

        @pl.when(kind == 1)
        def _():
            back_br.start()
            back_bl.start()
            back_tl.start()

    def window(i, carry):
        kind = lax.rem(core + i, 2)
        edge = jnp.where(kind == 0, lat == 15, lat == 0)
        arrive(kind, 0)
        clear(kind, 0, edge)

        x = buf[kind, 0].reshape(KC, D).astype(F32)
        centred = x - jnp.sum(x, axis=1, keepdims=True) * (1 / D)
        rstd = lax.rsqrt(jnp.sum(centred * centred, axis=1, keepdims=True) * (1 / D) + EPS)
        v = centred * rstd
        normed[...] = v
        rstd_s[...] = jnp.broadcast_to(rstd, (KC, 128))
        nl[0:KC, :] = (v * gain).astype(BF)
        q = (dot(w_t[0:D, :], nl[...], NT).astype(BF).astype(F32) * 0.125).astype(BF)
        qkv_t[0:6] = q.reshape(6, 64, QC)
        for part in (1, 2):
            rows = slice(part * D, (part + 1) * D)
            qkv_t[part * 6:part * 6 + 6] = dot(w_t[rows, :], nl[...], NT).astype(BF).reshape(6, 64, QC)
        arrive(kind, 1)
        clear(kind, 1, edge)

        @pl.when((i == 0) & (core == 0))
        def _():
            for n in range(2):
                halo_br[n].start()

        @pl.when((i == 0) & (core == 1))
        def _():
            for n in range(2):
                halo_a[n].start()
                halo_tl[n].start()
                halo_bl[n].start()

        gs[0:KC, :] = buf[kind, 1].reshape(KC, D)
        bt = dot(wp_ref[...], gs[...], NT).astype(BF).reshape(6, 64, QC)
        for h in range(HEADS):
            o = (h % 2) * 64
            q_aug[h, o:o + 64, :] = qkv_t[h]
            b_aug[h, o:o + 64, :] = bt[h]
        slot = jnp.where(kind == 0, row & 31, (row & 15) + 15)
        bad = (slot >= 30) | ((row >= KC // 2) & edge)
        bias = jnp.where((lane == 0) & bad, -30000.0, 0.0).astype(BF)
        for j in range(3):
            cols = slice(D + j * 128, D + (j + 1) * 128)
            k_aug[j, :, 0:128] = dot(nl[0:KC, :], w_ref[:, cols]).astype(BF)
            cols = slice(2 * D + j * 128, 2 * D + (j + 1) * 128)
            v_aug[j, :, 0:128] = dot(nl[0:KC, :], w_ref[:, cols]).astype(BF)
            k_aug[j, :, 128:256] = bias
        lax.fori_loop(0, HEADS, head, 0)
        dw = dot(dqkv_t[...].reshape(3 * D, QC), nl[...])
        for n in range(3):
            total[n, 0:1152, :] += dw[:, n * 128:(n + 1) * 128]
        gp[...] += dot(att_t[...].reshape(D, QC), gs[...])

        @pl.when(i == 0)
        def _():
            finish(kind)

        return carry

    lax.fori_loop(0, 2, window, 0)

    for n in range(3):
        total[n, 1152:1536, :] = gp[n * 128:(n + 1) * 128, :].T

    def gather(at_lon, j):
        first, step = (9 * at_lon + j, 72) if j < 9 else (1152 + 3 * at_lon + j - 9, 24)
        return jnp.concatenate([total[n, pl.ds(first, 16, stride=step), :] for n in range(3)], axis=1)

    turns = [lax.rem(y + k, 4) for k in (2, 1, 3, 0)]
    core_copies = [copy(core_send.at[i], core_recv.at[i], i, partner) for i in range(4)]
    for i in range(4):
        for j in range(12):
            core_send[i, j * 16:(j + 1) * 16, :] = gather(2 * turns[i] + 1 - core, j).astype(BF)
        core_copies[i].start()
    for i in range(4):
        for j in range(12):
            core_own[i, j * 16:(j + 1) * 16, :] = gather(2 * turns[i] + core, j)
    finish(1 - core)
    up, down = {"y": turns[1]}, {"y": turns[2]}
    y_copies = [copy(y_send.at[n], y_recv.at[n], 4 + n, (up, down)[n % 2]) for n in range(6)]
    first, second = slice(0, 96), slice(96, 192)

    def send_y(n, value):
        y_send[n] = value.astype(BF)
        y_copies[n].start()

    for i in range(4):
        core_copies[i].wait()
        core_own[i] = core_own[i] + core_recv[i].astype(F32)
        if i == 0:
            send_y(0, core_own[0, first])
            send_y(1, core_own[0, second])
        if i == 1:
            send_y(2, core_own[1, second])
        if i == 2:
            send_y(3, core_own[2, first])
    y_copies[0].wait()
    send_y(4, core_own[1, first] + y_recv[0].astype(F32))
    y_copies[1].wait()
    send_y(5, core_own[2, second] + y_recv[1].astype(F32))
    for n in range(2, 6):
        y_copies[n].wait()
    low = core_own[3, first] + y_recv[4].astype(F32) + y_recv[3].astype(F32)
    high = core_own[3, second] + y_recv[2].astype(F32) + y_recv[5].astype(F32)
    for n in range(3):
        y_own[n, first] = low[:, n * 128:(n + 1) * 128]
        y_own[n, second] = high[:, n * 128:(n + 1) * 128]

    def strided(first):
        return jnp.concatenate([y_own[n, pl.ds(first, 12, stride=16), :] for n in range(3)], axis=1)

    spare = jnp.zeros((4, D), F32)
    for t in range(16):
        lat_send[t] = jnp.concatenate([strided(t), spare], axis=0).astype(BF)
    lat_copies = []
    far_first = (4, 12, 3, 5, 11, 13, 2, 6, 10, 14, 1, 7, 9, 15, 8)
    for k in far_first:
        c = copy(lat_send.at[lax.rem(lat + k, 16)], lat_recv.at[k - 1], 9 + k, at(k, 0))
        c.start()
        lat_copies.append(c)
    back_tm.wait_recv()
    back_br.wait_recv()
    back_bl.wait_recv()
    back_tl.wait_recv()
    for i in range(15):
        for r, c0, c1, part in (
                (i, 0, 15, ret_tl[i, 0:15, :]), (i, 15, 45, ret_tm[i, 0:30, :]),
                (i, 45, 60, dbuf[1, 15 + i, 0:15, :]), (15 + i, 0, 15, ret_bl[i, 0:15, :]),
                (15 + i, 15, 45, dbuf[0, i, 0:30, :]), (15 + i, 45, 60, ret_br[i, 0:15, :])):
            out_ref[0, r, c0:c1, :] = (g_ref[r, c0:c1, :].astype(F32) + part.astype(F32)).astype(BF)
    own = strided(lat)
    for c, k in zip(lat_copies, far_first):
        c.wait()
        own = own + lat_recv[k - 1, 0:12, :].astype(F32)
    dp_send[...] = jnp.concatenate([own, spare], axis=0)
    c = copy(dp_send, dp_recv, 25, {"dp": 1 - dp})
    c.start()
    c.wait()
    factor = 460800.0 ** -0.5
    both = (dp_send[...] + dp_recv[...]) * factor
    mine = jnp.where(dp == 0, both, pltpu.roll(both, 192, 1))
    qkv_ref[...] = mine[0:9, 0:192]
    proj_ref[...] = mine[9:12, 0:192]
    for c in (*halo_a, *halo_br, *halo_tl, *halo_bl, back_tm, back_br, back_bl, back_tl):
        c.wait_send()


def per_device(hidden_in, grad_out, norm_gain, w_qkv, w_proj):
    V = pl.BlockSpec(memory_space=pltpu.VMEM)
    scratch = [
        ((30, 60, D), BF), ((30, 60, D), BF), ((D,), F32), ((D, 3 * D), BF), ((D, D), BF),
        ((2, 2, 30, 32, D), BF), ((2, 15, 32, D), BF), ((2, 15, 16, D), BF), ((2, 15, 16, D), BF),
        ((2, 15, 16, D), BF), ((2, 30, 32, D), BF), ((15, 32, D), BF), ((15, 16, D), BF), ((15, 16, D), BF),
        ((15, 16, D), BF),
        ((3 * D, D), BF), ((KC, D), F32), ((KC, 128), F32), ((QC, D), BF), ((QC, D), BF), ((6, 256, QC), BF),
        ((6, 256, QC), BF), ((3, KC, 256), BF), ((3, KC, 256), BF), ((18, 64, QC), BF), ((KC, QC), F32),
        ((KC, QC), BF), ((KC, QC), BF), ((18, 64, QC), BF), ((6, 64, QC), BF),
        ((D, D), F32), ((3, 1536, 128), F32), ((4, 192, D), BF), ((4, 192, D), BF), ((4, 192, D), F32),
        ((6, 96, D), BF), ((6, 96, D), BF), ((3, 192, 128), F32), ((16, 16, D), BF), ((15, 16, D), BF),
        ((16, D), F32), ((16, D), F32),
    ]
    H = pl.BlockSpec(memory_space=pltpu.HBM)
    args = [pltpu.with_memory_space_constraint(a, pltpu.HBM)
            for a in (hidden_in, grad_out, norm_gain, w_qkv, w_proj)]
    grad_in, qkv, proj = pl.pallas_call(
        kernel,
        out_shape=(jax.ShapeDtypeStruct(grad_out.shape, BF), jax.ShapeDtypeStruct((9, 192), F32),
                   jax.ShapeDtypeStruct((3, 192), F32)),
        in_specs=[H] * 5,
        out_specs=(V, V, V),
        scratch_shapes=[pltpu.VMEM(s, d) for s, d in scratch] + [pltpu.SemaphoreType.DMA((38,))] * 2
        + [pltpu.SemaphoreType.DMA((5,))],
        compiler_params=pltpu.CompilerParams(
            vmem_limit_bytes=50 * 1024 * 1024, collective_id=0, has_side_effects=True),
        name="block_backward",
    )(*args)
    return grad_in, qkv.T, proj.T


def solution(mesh):
    split = Mesh(mesh.devices.reshape(2, 2, 8, 4, 2), ("dp", "xl", "z", "y", "core"))
    return jax.shard_map(
        per_device,
        mesh=split,
        in_specs=(P("dp", LAT, LON, None), P("dp", LAT, LON, None), P(), P(), P()),
        out_specs=(P("dp", LAT, LON, None), P("dp", BOTH), P("dp", BOTH)),
        check_vma=False,
    )
```

```python
import jax
import jax.numpy as jnp
from jax import lax
from jax.experimental import pallas as pl
from jax.experimental.pallas import tpu as pltpu
from jax.sharding import Mesh
from jax.sharding import PartitionSpec as P

HEADS = 6
D = 384
EPS = 1e-5
KC = 960
QC = 1024
CK = 480
BF = jnp.bfloat16
F32 = jnp.float32
MESH = pl.DeviceIdType.MESH
NN = (((1,), (0,)), ((), ()))
NT = (((1,), (1,)), ((), ()))
LAT = ("xl", "z")
LON = ("y", "core")
BOTH = LAT + LON


def dot(a, b, dims=NN):
    return lax.dot_general(a, b, dims, preferred_element_type=F32)


def kernel(x_hbm, g_hbm, gain_hbm, w_hbm, wp_hbm, out_ref, qkv_ref, proj_ref,
           x_ref, g_ref, gain_ref, w_ref, wp_ref,
           buf, s_a, s_br, s_tl, s_bl, dbuf, ret_tm, ret_br, ret_bl, ret_tl,
           w_t, normed, rstd_s, nl, gs, q_aug, b_aug, k_aug, v_aug, qkv_t, p32, p_low, ds_low, dqkv_t, att_t,
           gp, total, core_send, core_recv, core_own, y_send, y_recv, y_own, lat_send, lat_recv,
           dp_send, dp_recv, send_sems, recv_sems, load_sems):
    dp, xl, z, y, core = (lax.axis_index(n) for n in ("dp", "xl", "z", "y", "core"))
    loads = [pltpu.make_async_copy(src, dst, load_sems.at[n]) for n, (src, dst) in enumerate((
        (x_hbm.at[0], x_ref), (g_hbm.at[0], g_ref), (w_hbm, w_ref), (wp_hbm, wp_ref), (gain_hbm, gain_ref)))]
    for load in loads:
        load.start()
    lat = xl * 8 + z
    lon = y * 2 + core

    def at(lat_by, lon_by):
        t = lax.rem(lat + lat_by + 16, 16)
        u = lax.rem(lon + lon_by + 8, 8)
        return {"xl": t // 8, "z": lax.rem(t, 8), "y": u // 2, "core": lax.rem(u, 2)}

    def copy(src, dst, number, peer):
        return pltpu.make_async_remote_copy(
            src_ref=src, dst_ref=dst, send_sem=send_sems.at[number], recv_sem=recv_sems.at[number],
            device_id=peer, device_id_type=MESH)

    barrier = pltpu.get_barrier_semaphore()
    partner = {"core": 1 - core}
    peers = [partner, {"dp": 1 - dp}, at(0, -1), at(0, 1), at(1, -1), at(-1, 1)]
    peers += [{"y": lax.rem(y + k, 4)} for k in range(1, 4)]
    peers += [at(k, 0) for k in range(1, 16)]
    for peer in peers:
        pl.semaphore_signal(barrier, inc=1, device_id=peer, device_id_type=MESH)

    halo_a = [copy(s_a.at[n], buf.at[0, n, 15:30], 26 + n, at(-1, 0)) for n in range(2)]
    halo_br = [copy(s_br.at[n], buf.at[1, n, 0:15, 0:16], 28 + n, at(1, 0)) for n in range(2)]
    halo_tl = [copy(s_tl.at[n], buf.at[1, n, 15:30, 16:32], 30 + n, at(0, -1)) for n in range(2)]
    halo_bl = [copy(s_bl.at[n], buf.at[1, n, 0:15, 16:32], 32 + n, at(1, -1)) for n in range(2)]
    back_tm = copy(dbuf.at[0, 15:30], ret_tm, 34, at(1, 0))
    back_br = copy(dbuf.at[1, 0:15, 0:16], ret_br, 35, at(-1, 0))
    back_bl = copy(dbuf.at[1, 0:15, 16:32], ret_bl, 36, at(-1, 1))
    back_tl = copy(dbuf.at[1, 15:30, 16:32], ret_tl, 37, at(0, 1))

    pad1 = jnp.zeros((1, D), BF)
    pad2 = jnp.zeros((2, D), BF)
    for n, ref in ((0, x_ref), (1, g_ref)):
        loads[n].wait()
        for i in range(15):
            s_a[n, i, 0:30, :] = ref[i, 15:45, :]
            s_a[n, i, 30:32, :] = pad2
            s_tl[n, i, 0:15, :] = ref[i, 0:15, :]
            s_tl[n, i, 15:16, :] = pad1
            s_br[n, i, 0:15, :] = ref[15 + i, 45:60, :]
            s_br[n, i, 15:16, :] = pad1
            s_bl[n, i, 0:15, :] = ref[15 + i, 0:15, :]
            s_bl[n, i, 15:16, :] = pad1
        if n == 0:
            pl.semaphore_wait(barrier, len(peers))

        @pl.when(core == 0)
        def _():
            halo_a[n].start()
            halo_tl[n].start()
            halo_bl[n].start()

        @pl.when(core == 1)
        def _():
            halo_br[n].start()

    for n, ref in ((0, x_ref), (1, g_ref)):
        for i in range(15):
            buf[0, n, i, 0:30, :] = ref[15 + i, 15:45, :]
            buf[0, n, i, 30:32, :] = pad2
            buf[1, n, 15 + i, 0:15, :] = ref[i, 45:60, :]
            buf[1, n, 15 + i, 15:16, :] = pad1

    for load in loads[2:]:
        load.wait()
    gain = gain_ref[...].reshape(1, D)
    for n in range(9):
        w_t[n * 128:(n + 1) * 128, :] = w_ref[:, n * 128:(n + 1) * 128].T
    gp[...] = jnp.zeros_like(gp)
    for n in range(3):
        total[n, 0:1152, :] = jnp.zeros((1152, 128), F32)
    nl[KC:, :] = jnp.zeros((QC - KC, D), BF)
    gs[KC:, :] = jnp.zeros((QC - KC, D), BF)
    dqkv_t[:, :, KC:] = jnp.zeros((18, 64, QC - KC), BF)
    half = jnp.zeros((64, QC), BF)
    one = (lax.broadcasted_iota(jnp.int32, (128, QC), 0) == 0).astype(F32).astype(BF)
    rest = jnp.zeros((128, QC), BF)
    for h in range(HEADS):
        o = (h % 2) * 64
        q_aug[h, 64 - o:128 - o, :] = half
        b_aug[h, 64 - o:128 - o, :] = half
        q_aug[h, 128:256, :] = one
        b_aug[h, 128:256, :] = rest
    row = lax.broadcasted_iota(jnp.int32, (KC, 128), 0)
    lane = lax.broadcasted_iota(jnp.int32, (KC, 128), 1)
    ones = jnp.where(lane < 2, 1.0, 0.0).astype(BF)
    for j in range(3):
        v_aug[j, :, 128:256] = ones

    def scores(j, u):
        acc = jnp.zeros((8, QC), F32)
        for k in range(0, KC, CK):
            e = jnp.exp(dot(k_aug[j, k:k + CK, :], q_aug[2 * j + u]))
            p32[u, k:k + CK, :] = e
            acc = acc + jnp.sum(e.reshape(CK // 8, 8, QC), axis=0)
        return 1.0 / jnp.sum(acc, axis=0, keepdims=True)

    def normalise(u, r):
        for k in range(0, KC, CK):
            p = p32[u, k:k + CK, :] * r
            p32[u, k:k + CK, :] = p
            p_low[u, k:k + CK, :] = p.astype(BF)

    def attend(j, u):
        h, o = 2 * j + u, 64 * u
        a = dot(qkv_t[12 + h][:, 0:KC], p_low[u])
        att_t[h] = a.astype(BF)
        less = -jnp.sum(a * b_aug[h, o:o + 64, :].astype(F32), axis=0, keepdims=True)
        high = less.astype(BF).astype(F32)
        r16 = lax.broadcasted_iota(jnp.int32, (16, QC), 0)
        b_aug[h, 128:144, :] = jnp.where(r16 == 0, high, jnp.where(r16 == 1, less - high, 0.0)).astype(BF)

    def score_grads(j, u):
        for k in range(0, KC, CK):
            dprobs = dot(v_aug[j, k:k + CK, :], b_aug[2 * j + u])
            ds_low[u, k:k + CK, :] = (p32[u, k:k + CK, :] * dprobs).astype(BF)

    def value_grads(j, u):
        h, o = 2 * j + u, 64 * u
        dqkv_t[12 + h, :, 0:KC] = dot(b_aug[h, o:o + 64, :], p_low[u], NT).astype(BF)

    def query_grads(j, u):
        h = 2 * j + u
        dqkv_t[h] = (dot(qkv_t[6 + h][:, 0:KC], ds_low[u]) * 0.125).astype(BF)

    def key_grads(j, u):
        h = 2 * j + u
        dqkv_t[6 + h, :, 0:KC] = dot(qkv_t[h], ds_low[u], NT).astype(BF)

    def pair(j, carry):
        r0 = scores(j, 0)
        r1 = scores(j, 1)
        for u, r in ((0, r0), (1, r1)):
            normalise(u, r)
            attend(j, u)
        for step in (score_grads, value_grads, query_grads, key_grads):
            step(j, 0)
            step(j, 1)
        return carry

    def arrive(kind, n):
        @pl.when(kind == 0)
        def _():
            halo_a[n].wait_recv()

        @pl.when(kind == 1)
        def _():
            halo_br[n].wait_recv()
            halo_tl[n].wait_recv()
            halo_bl[n].wait_recv()

    def clear(kind, n, edge):
        @pl.when(edge)
        def _():
            buf[kind, n, 15:30, :, :] = jnp.zeros((15, 32, D), BF)

    def finish(kind):
        for t in range(4):
            n = 256 if t < 3 else 192
            rows = slice(t * 256, t * 256 + 256)
            dn = dot(w_ref[...], dqkv_t[:, :, rows].reshape(3 * D, 256)).T[0:n] * gain
            own = slice(t * 256, t * 256 + n)
            norm = normed[own, :]
            m1 = jnp.sum(dn, axis=1, keepdims=True) * (1 / D)
            m2 = jnp.sum(dn * norm, axis=1, keepdims=True) * (1 / D)
            d = (rstd_s[own, 0:1] * (dn - m1 - norm * m2)).astype(BF)
            dbuf[kind, t * 8:t * 8 + n // 32] = d.reshape(n // 32, 32, D)

        @pl.when(kind == 0)
        def _():
            back_tm.start()

        @pl.when(kind == 1)
        def _():
            back_br.start()
            back_bl.start()
            back_tl.start()

    def window(i, carry):
        kind = lax.rem(core + i, 2)
        edge = jnp.where(kind == 0, lat == 15, lat == 0)
        arrive(kind, 0)
        clear(kind, 0, edge)

        x = buf[kind, 0].reshape(KC, D).astype(F32)
        centred = x - jnp.sum(x, axis=1, keepdims=True) * (1 / D)
        rstd = lax.rsqrt(jnp.sum(centred * centred, axis=1, keepdims=True) * (1 / D) + EPS)
        v = centred * rstd
        normed[...] = v
        rstd_s[...] = jnp.broadcast_to(rstd, (KC, 128))
        nl[0:KC, :] = (v * gain).astype(BF)
        q = (dot(w_t[0:D, :], nl[...], NT).astype(BF).astype(F32) * 0.125).astype(BF)
        qkv_t[0:6] = q.reshape(6, 64, QC)
        for part in (1, 2):
            rows = slice(part * D, (part + 1) * D)
            qkv_t[part * 6:part * 6 + 6] = dot(w_t[rows, :], nl[...], NT).astype(BF).reshape(6, 64, QC)
        arrive(kind, 1)
        clear(kind, 1, edge)

        @pl.when((i == 0) & (core == 0))
        def _():
            for n in range(2):
                halo_br[n].start()

        @pl.when((i == 0) & (core == 1))
        def _():
            for n in range(2):
                halo_a[n].start()
                halo_tl[n].start()
                halo_bl[n].start()

        gs[0:KC, :] = buf[kind, 1].reshape(KC, D)
        bt = dot(wp_ref[...], gs[...], NT).astype(BF).reshape(6, 64, QC)
        for h in range(HEADS):
            o = (h % 2) * 64
            q_aug[h, o:o + 64, :] = qkv_t[h]
            b_aug[h, o:o + 64, :] = bt[h]
        slot = jnp.where(kind == 0, row & 31, (row & 15) + 15)
        bad = (slot >= 30) | ((row >= KC // 2) & edge)
        bias = jnp.where((lane == 0) & bad, -30000.0, 0.0).astype(BF)
        for j in range(3):
            cols = slice(D + j * 128, D + (j + 1) * 128)
            k_aug[j, :, 0:128] = dot(nl[0:KC, :], w_ref[:, cols]).astype(BF)
            cols = slice(2 * D + j * 128, 2 * D + (j + 1) * 128)
            v_aug[j, :, 0:128] = dot(nl[0:KC, :], w_ref[:, cols]).astype(BF)
            k_aug[j, :, 128:256] = bias
        lax.fori_loop(0, HEADS // 2, pair, 0)
        dw = dot(dqkv_t[...].reshape(3 * D, QC), nl[...])
        for n in range(3):
            total[n, 0:1152, :] += dw[:, n * 128:(n + 1) * 128]
        gp[...] += dot(att_t[...].reshape(D, QC), gs[...])

        @pl.when(i == 0)
        def _():
            finish(kind)

        return carry

    lax.fori_loop(0, 2, window, 0)

    for n in range(3):
        total[n, 1152:1536, :] = gp[n * 128:(n + 1) * 128, :].T

    def gather(at_lon, j):
        first, step = (9 * at_lon + j, 72) if j < 9 else (1152 + 3 * at_lon + j - 9, 24)
        return jnp.concatenate([total[n, pl.ds(first, 16, stride=step), :] for n in range(3)], axis=1)

    turns = [lax.rem(y + k, 4) for k in (2, 1, 3, 0)]
    core_copies = [copy(core_send.at[i], core_recv.at[i], i, partner) for i in range(4)]
    for i in range(4):
        for j in range(12):
            core_send[i, j * 16:(j + 1) * 16, :] = gather(2 * turns[i] + 1 - core, j).astype(BF)
        core_copies[i].start()
    for i in range(4):
        for j in range(12):
            core_own[i, j * 16:(j + 1) * 16, :] = gather(2 * turns[i] + core, j)
    finish(1 - core)
    up, down = {"y": turns[1]}, {"y": turns[2]}
    y_copies = [copy(y_send.at[n], y_recv.at[n], 4 + n, (up, down)[n % 2]) for n in range(6)]
    first, second = slice(0, 96), slice(96, 192)

    def send_y(n, value):
        y_send[n] = value.astype(BF)
        y_copies[n].start()

    for i in range(4):
        core_copies[i].wait()
        core_own[i] = core_own[i] + core_recv[i].astype(F32)
        if i == 0:
            send_y(0, core_own[0, first])
            send_y(1, core_own[0, second])
        if i == 1:
            send_y(2, core_own[1, second])
        if i == 2:
            send_y(3, core_own[2, first])
    y_copies[0].wait()
    send_y(4, core_own[1, first] + y_recv[0].astype(F32))
    y_copies[1].wait()
    send_y(5, core_own[2, second] + y_recv[1].astype(F32))
    for n in range(2, 6):
        y_copies[n].wait()
    low = core_own[3, first] + y_recv[4].astype(F32) + y_recv[3].astype(F32)
    high = core_own[3, second] + y_recv[2].astype(F32) + y_recv[5].astype(F32)
    for n in range(3):
        y_own[n, first] = low[:, n * 128:(n + 1) * 128]
        y_own[n, second] = high[:, n * 128:(n + 1) * 128]

    def strided(first):
        return jnp.concatenate([y_own[n, pl.ds(first, 12, stride=16), :] for n in range(3)], axis=1)

    spare = jnp.zeros((4, D), F32)
    for t in range(16):
        lat_send[t] = jnp.concatenate([strided(t), spare], axis=0).astype(BF)
    lat_copies = []
    far_first = (4, 12, 3, 5, 11, 13, 2, 6, 10, 14, 1, 7, 9, 15, 8)
    for k in far_first:
        c = copy(lat_send.at[lax.rem(lat + k, 16)], lat_recv.at[k - 1], 9 + k, at(k, 0))
        c.start()
        lat_copies.append(c)
    back_tm.wait_recv()
    back_br.wait_recv()
    back_bl.wait_recv()
    back_tl.wait_recv()
    for i in range(15):
        for r, c0, c1, part in (
                (i, 0, 15, ret_tl[i, 0:15, :]), (i, 15, 45, ret_tm[i, 0:30, :]),
                (i, 45, 60, dbuf[1, 15 + i, 0:15, :]), (15 + i, 0, 15, ret_bl[i, 0:15, :]),
                (15 + i, 15, 45, dbuf[0, i, 0:30, :]), (15 + i, 45, 60, ret_br[i, 0:15, :])):
            out_ref[0, r, c0:c1, :] = (g_ref[r, c0:c1, :].astype(F32) + part.astype(F32)).astype(BF)
    own = strided(lat)
    for c, k in zip(lat_copies, far_first):
        c.wait()
        own = own + lat_recv[k - 1, 0:12, :].astype(F32)
    dp_send[...] = jnp.concatenate([own, spare], axis=0)
    c = copy(dp_send, dp_recv, 25, {"dp": 1 - dp})
    c.start()
    c.wait()
    factor = 460800.0 ** -0.5
    both = (dp_send[...] + dp_recv[...]) * factor
    mine = jnp.where(dp == 0, both, pltpu.roll(both, 192, 1))
    qkv_ref[...] = mine[0:9, 0:192]
    proj_ref[...] = mine[9:12, 0:192]
    for c in (*halo_a, *halo_br, *halo_tl, *halo_bl, back_tm, back_br, back_bl, back_tl):
        c.wait_send()


def per_device(hidden_in, grad_out, norm_gain, w_qkv, w_proj):
    V = pl.BlockSpec(memory_space=pltpu.VMEM)
    scratch = [
        ((30, 60, D), BF), ((30, 60, D), BF), ((D,), F32), ((D, 3 * D), BF), ((D, D), BF),
        ((2, 2, 30, 32, D), BF), ((2, 15, 32, D), BF), ((2, 15, 16, D), BF), ((2, 15, 16, D), BF),
        ((2, 15, 16, D), BF), ((2, 30, 32, D), BF), ((15, 32, D), BF), ((15, 16, D), BF), ((15, 16, D), BF),
        ((15, 16, D), BF),
        ((3 * D, D), BF), ((KC, D), F32), ((KC, 128), F32), ((QC, D), BF), ((QC, D), BF), ((6, 256, QC), BF),
        ((6, 256, QC), BF), ((3, KC, 256), BF), ((3, KC, 256), BF), ((18, 64, QC), BF), ((2, KC, QC), F32),
        ((2, KC, QC), BF), ((2, KC, QC), BF), ((18, 64, QC), BF), ((6, 64, QC), BF),
        ((D, D), F32), ((3, 1536, 128), F32), ((4, 192, D), BF), ((4, 192, D), BF), ((4, 192, D), F32),
        ((6, 96, D), BF), ((6, 96, D), BF), ((3, 192, 128), F32), ((16, 16, D), BF), ((15, 16, D), BF),
        ((16, D), F32), ((16, D), F32),
    ]
    H = pl.BlockSpec(memory_space=pltpu.HBM)
    args = [pltpu.with_memory_space_constraint(a, pltpu.HBM)
            for a in (hidden_in, grad_out, norm_gain, w_qkv, w_proj)]
    grad_in, qkv, proj = pl.pallas_call(
        kernel,
        out_shape=(jax.ShapeDtypeStruct(grad_out.shape, BF), jax.ShapeDtypeStruct((9, 192), F32),
                   jax.ShapeDtypeStruct((3, 192), F32)),
        in_specs=[H] * 5,
        out_specs=(V, V, V),
        scratch_shapes=[pltpu.VMEM(s, d) for s, d in scratch] + [pltpu.SemaphoreType.DMA((38,))] * 2
        + [pltpu.SemaphoreType.DMA((5,))],
        compiler_params=pltpu.CompilerParams(
            vmem_limit_bytes=52 * 1024 * 1024, collective_id=0, has_side_effects=True),
        name="block_backward",
    )(*args)
    return grad_in, qkv.T, proj.T


def solution(mesh):
    split = Mesh(mesh.devices.reshape(2, 2, 8, 4, 2), ("dp", "xl", "z", "y", "core"))
    return jax.shard_map(
        per_device,
        mesh=split,
        in_specs=(P("dp", LAT, LON, None), P("dp", LAT, LON, None), P(), P(), P()),
        out_specs=(P("dp", LAT, LON, None), P("dp", BOTH), P("dp", BOTH)),
        check_vma=False,
    )
```
